512 devices in a mesh: ctx: 32 (over z, x), tp: 8 (over y), pp: 2 (over core).
Axes of the slice: x: 4, y: 8, z: 8, core: 2. Of those that a mesh axis runs over, the one named last changes fastest.
Arguments:
- features: bfloat16 [2, 8192, 3, 8192], P('pp', 'ctx', None, 'tp'), may hold values from -6 to 6
- short_taps: float32 [2, 3, 3, 8192], P('pp', None, None, 'tp'), may hold values from -3 to 3
- long_filters: bfloat16 [2, 128, 512], P('pp', None, 'tp'), may hold values from -0.5 to 0.5
- out_weight: bfloat16 [2, 8192, 4096], P('pp', 'tp', 'ctx'), may hold values from -0.09375 to 0.09375
- out_grad: bfloat16 [2, 8192, 4096], P('pp', 'ctx', 'tp'), may hold values from -6 to 6
Outputs:
- received_adjoint: bfloat16 [2, 8192, 3, 8192], P('pp', 'ctx', None, 'tp')
The draws below stay inside these ranges and needn't reach their ends.
All inputs are finite; a program needn't handle non-finite values.
Results may differ from the reference program's by a relative error of at most 0.013.
Values may be sent and summed in bfloat16 or wider, within the bound.
No kernel may reach another device: no remote copies, remote signals or barrier semaphores. Data moves between devices by JAX's collectives and lax.ppermute only.
A program may use at most 128 MiB of HBM per device.

```python
import jax
import jax.numpy as jnp
from jax import lax

D = 8192
GROUP_CH = 16
FILT = 128
DOUT = 4096
GROUPS = 512
TOKENS = 8192
SECTIONS = 2


def levels(stream_key, shape, cuts, smallest, high):
    gain, own = 1.0, jax.random.fold_in(stream_key, 6)
    for dim, blocks in cuts:
        heights = jnp.exp(jax.random.uniform(jax.random.fold_in(own, dim), (blocks,), jnp.float32, smallest / len(cuts), high / len(cuts)))
        gain = gain * jnp.repeat(heights, shape[dim] // blocks).reshape([-1 if axis == dim else 1 for axis in range(len(shape))])
    return gain


def scatter_about(key, extent, scale, most, cuts=(), held_as=jnp.bfloat16):
    entries = scale * jax.random.normal(key, extent, jnp.float32)
    if cuts:
        entries = entries * levels(key, extent, cuts, -0.22, 0.18)
    return jnp.clip(entries, -most, most).astype(held_as)


def setup_inputs(seed: int = 0) -> dict:
    key_list = jax.random.split(jax.random.key(seed), 6)
    features = scatter_about(key_list[0], (SECTIONS, TOKENS, 3, D), 1.0, 6.0, ((0, 2), (1, 32), (3, 8)))
    short_taps = scatter_about(key_list[1], (SECTIONS, 3, 3, D), 0.6, 3.0, ((0, 2), (3, 8)), jnp.float32)
    long_filters = scatter_about(key_list[2], (SECTIONS, FILT, GROUPS), 0.09, 0.5, ((0, 2), (2, 8)))
    out_weight = scatter_about(key_list[3], (SECTIONS, D, DOUT), DOUT ** -0.5, 0.09375, ((0, 2), (1, 8), (2, 32)))
    out_grad = scatter_about(key_list[4], (SECTIONS, TOKENS, DOUT), 1.0, 6.0, ((0, 2), (1, 32), (2, 8)))
    return dict(features=features, short_taps=short_taps, long_filters=long_filters, out_weight=out_weight, out_grad=out_grad)


def one_section(feats, short_taps, filters, weight, cotangent):
    count = feats.shape[0]
    feat_f = feats.astype(jnp.float32)
    padded = jnp.pad(feat_f, ((2, 0), (0, 0), (0, 0)))
    mixed = short_taps[0] * padded[2:] + short_taps[1] * padded[1:-1] + short_taps[2] * padded[:-2]
    gate_part = mixed[:, 0]
    key_part = mixed[:, 1]
    value_part = mixed[:, 2]
    products = (key_part * value_part).astype(jnp.bfloat16)
    filt_chan = jnp.repeat(filters.astype(jnp.float32), GROUP_CH, axis=1)
    prod_pad = jnp.pad(products.astype(jnp.float32), ((FILT - 1, 0), (0, 0)))

    def fwd_tap(j, acc):
        return acc + filt_chan[j] * lax.dynamic_slice_in_dim(prod_pad, FILT - 1 - j, count, 0)

    conv_out = lax.fori_loop(0, FILT, fwd_tap, jnp.zeros(gate_part.shape, jnp.float32))
    grad_y = jnp.dot(cotangent, weight.T, preferred_element_type=jnp.float32).astype(jnp.bfloat16)
    grad_yf = grad_y.astype(jnp.float32)
    grad_gate = grad_yf * conv_out
    grad_conv = (grad_yf * gate_part).astype(jnp.bfloat16)
    conv_pad = jnp.pad(grad_conv.astype(jnp.float32), ((0, FILT - 1), (0, 0)))

    def bwd_tap(j, acc):
        return acc + filt_chan[j] * lax.dynamic_slice_in_dim(conv_pad, j, count, 0)

    grad_prod = lax.fori_loop(0, FILT, bwd_tap, jnp.zeros(gate_part.shape, jnp.float32))
    grad_mix = jnp.stack([grad_gate, grad_prod * value_part, grad_prod * key_part], axis=1).astype(jnp.bfloat16)
    mix_pad = jnp.pad(grad_mix.astype(jnp.float32), ((0, 2), (0, 0), (0, 0)))
    grad_feat = short_taps[0] * mix_pad[:count] + short_taps[1] * mix_pad[1:count + 1] + short_taps[2] * mix_pad[2:]
    return grad_feat.astype(jnp.bfloat16)


def reference(features, short_taps, long_filters, out_weight, out_grad):
    results = []
    for section in range(SECTIONS):
        results.append(one_section(features[section], short_taps[section], long_filters[section], out_weight[section], out_grad[section]))
    return jnp.stack([results[(section + 1) % SECTIONS] for section in range(SECTIONS)])
```

```python
import jax
import jax.numpy as jnp
from jax import lax
from jax.experimental import pallas as pl
from jax.experimental.pallas import tpu as pltpu
from jax.sharding import PartitionSpec as P

BF = jnp.bfloat16
F32 = jnp.float32
LANES = 128
X = 4
RING = 8
HALO = 144


def vmem(n):
    return [pl.BlockSpec(memory_space=pltpu.VMEM)] * n


def params(mib):
    return pltpu.CompilerParams(vmem_limit_bytes=mib << 20)


def pair_tp(v, parity):
    return lax.ppermute(v, "tp", [(i, partner(i, parity)) for i in range(RING)])


def pair_z(v, parity):
    route = []
    for i in range(RING):
        for x in range(X):
            route.append((i * X + x, partner(i, parity) * X + x))
    return lax.ppermute(v, "ctx", route)


def pair_x(v, flip):
    return lax.ppermute(v, "ctx", [(c, c ^ flip) for c in range(RING * X)])


def shift_ctx(v, by):
    n = RING * X
    return lax.ppermute(v, "ctx", [(i, i + by) for i in range(n) if 0 <= i + by < n])


def partner(i, parity):
    return (i + 1) % RING if i % 2 == parity else (i - 1) % RING


def gather_halves(halves, exchange):
    held = []
    for parity, own in enumerate(halves):
        first = exchange(own, parity)
        second = exchange(jnp.stack([own, first]), 1 - parity)
        third = exchange(second, parity)
        fourth = exchange(third, 1 - parity)
        held.append([own, first, second, third, fourth])
    return held


def place(refs, full_ref, me):
    half_rows = full_ref.shape[0] // 2
    for half in range(2):
        own, first, second, third, fourth = refs[5 * half : 5 * half + 5]
        step = jnp.where(lax.rem(me, 2) == half, 1, -1)
        rows = pl.ds(half * half_rows, half_rows)

        def put(value, index):
            at = pl.multiple_of(lax.rem(index + 2 * RING, RING) * LANES, LANES)
            full_ref[rows, pl.ds(at, LANES)] = value

        put(own[...], me)
        put(first[...], me + step)
        put(second[0], me - step)
        put(second[1], me - 2 * step)
        put(third[0], me + 2 * step)
        put(third[1], me + 3 * step)
        put(fourth[0], me - 3 * step)
        put(fourth[1], me - 4 * step)


def matmul_kernel(*refs):
    a_refs, b_refs = refs[:10], refs[10:20]
    send0, send1, keep0, keep1, a_full, b_full = refs[20:]
    ctx = lax.axis_index("ctx")
    z, x = ctx // X, lax.rem(ctx, X)
    place(a_refs, a_full, lax.axis_index("tp"))
    place(b_refs, b_full, z)
    rows = a_full.shape[0] // X
    cols = b_full.shape[0] // 2
    flip1 = x + 1 - 2 * lax.rem(x, 2)
    flip3 = 3 - x
    flip2 = 3 - flip1

    def part(dest, half):
        at = pl.multiple_of(dest * rows, rows)
        return lax.dot_general(
            a_full[pl.ds(at, rows), :],
            b_full[half * cols : (half + 1) * cols, :],
            (((1,), (1,)), ((), ())),
            preferred_element_type=F32,
        )

    send0[0] = part(flip1, 0).astype(BF)
    send0[1] = part(flip2, 0).astype(BF)
    send1[0] = part(flip3, 1).astype(BF)
    send1[1] = part(flip2, 1).astype(BF)
    keep0[0] = part(x, 0)
    keep0[1] = part(flip3, 0)
    keep1[0] = part(x, 1)
    keep1[1] = part(flip1, 1)


def partial_products(a_held, b_held):
    rows = 2 * a_held[0][0].shape[0]
    cols = 2 * b_held[0][0].shape[0]
    depth = RING * LANES
    shape = (2, rows // X, cols // 2)
    return pl.pallas_call(
        matmul_kernel,
        out_shape=[jax.ShapeDtypeStruct(shape, BF)] * 2 + [jax.ShapeDtypeStruct(shape, F32)] * 2,
        in_specs=vmem(20),
        out_specs=vmem(4),
        scratch_shapes=[pltpu.VMEM((rows, depth), BF), pltpu.VMEM((cols, depth), BF)],
        compiler_params=params(24),
        cost_estimate=pl.CostEstimate(
            flops=2 * rows * cols * depth, bytes_accessed=12 << 20, transcendentals=0
        ),
        name="partial_products",
    )(*a_held[0], *a_held[1], *b_held[0], *b_held[1])


def lane_tile(index):
    return pl.ds(pl.multiple_of(index * LANES, LANES), LANES)


def tail_kernel(feats, taps, out, ext):
    rows = feats.shape[1]
    keep = rows - LANES

    def tile(l, carry):
        at = lane_tile(l)
        mixed = []
        for i in (1, 2):
            ext[...] = feats[i, keep - 16 : rows, at].astype(F32)
            mixed.append(
                taps[i : i + 1, at] * ext[16 : 16 + LANES]
                + taps[3 + i : 4 + i, at] * ext[15 : 15 + LANES]
                + taps[6 + i : 7 + i, at] * ext[14 : 14 + LANES]
            )
        out[0:LANES, at] = (mixed[0] * mixed[1]).astype(BF)
        last = [feats[i, rows - 16 : rows, at].astype(F32)[14:16] for i in range(3)]
        last.append(jnp.zeros((10, LANES), F32))
        out[LANES:HALO, at] = jnp.concatenate(last, axis=0).astype(BF)
        return carry

    lax.fori_loop(0, feats.shape[2] // LANES, tile, 0)


def tail_rows(feats, taps):
    channels = feats.shape[2]
    return pl.pallas_call(
        tail_kernel,
        out_shape=jax.ShapeDtypeStruct((HALO, channels), BF),
        in_specs=vmem(2),
        out_specs=vmem(1)[0],
        scratch_shapes=[pltpu.VMEM((LANES + 16, LANES), F32)],
        compiler_params=params(8),
        cost_estimate=pl.CostEstimate(flops=1 << 20, bytes_accessed=2 << 20, transcendentals=0),
        name="tail_rows",
    )(feats, taps)


def pick_groups(product, per_tile, width):
    rows = product.shape[0] // per_tile
    shape = (rows, product.shape[1])
    group = lax.rem(lax.broadcasted_iota(jnp.int32, shape, 1), LANES) // width
    out = product[:rows]
    for g in range(1, per_tile):
        out = jnp.where(group == g, product[g * rows : (g + 1) * rows], out)
    return out


def forward_kernel(feats, taps, filters, halo, conv, gate, key, value, back, fwd_band, flipped, plain, ext):
    rows = feats.shape[1]
    groups = filters.shape[0]
    per_tile = groups * LANES // feats.shape[2]
    width = LANES // per_tile
    row = lax.broadcasted_iota(jnp.int32, (LANES, LANES), 0)
    col = lax.broadcasted_iota(jnp.int32, (LANES, LANES), 1)
    mirror = jnp.where(lax.rem(row + col, LANES) == 0, 1.0, 0.0).astype(BF)
    flipped[...] = jnp.dot(filters[...], mirror, preferred_element_type=F32)
    plain[...] = filters[...].astype(F32)

    def tile(l, carry):
        at = lane_tile(l)
        for g in range(per_tile):
            index = l * per_tile + g
            spread = jnp.broadcast_to(plain[pl.ds(index, 1), :], (LANES, LANES))
            turned = pltpu.roll(spread, 0, 1, stride=1, stride_axis=0)
            back[index, :, 0:LANES] = jnp.where(col >= row, turned, 0.0).astype(BF)
            back[index, :, LANES : 2 * LANES] = jnp.where(col < row, turned, 0.0).astype(BF)
            spread = jnp.broadcast_to(flipped[pl.ds(index, 1), :], (LANES, LANES))
            turned = pltpu.roll(spread, 0, 1, stride=1, stride_axis=0)
            fwd_band[g * LANES : (g + 1) * LANES, 0:LANES] = jnp.where(col > row, turned, 0.0).astype(BF)
            fwd_band[g * LANES : (g + 1) * LANES, LANES : 2 * LANES] = jnp.where(
                col <= row, turned, 0.0
            ).astype(BF)
        before = halo[LANES:HALO, at].astype(F32)
        mixed = []
        for i in range(3):
            ext[0:8] = jnp.concatenate([jnp.zeros((6, LANES), F32), before[2 * i : 2 * i + 2]], axis=0)
            ext[8 : 8 + rows] = feats[i, :, at].astype(F32)
            mixed.append(
                taps[i : i + 1, at] * ext[8 : 8 + rows]
                + taps[3 + i : 4 + i, at] * ext[7 : 7 + rows]
                + taps[6 + i : 7 + i, at] * ext[6 : 6 + rows]
            )
        gate[:, at] = mixed[0]
        key[:, at] = mixed[1]
        value[:, at] = mixed[2]
        products = (mixed[1] * mixed[2]).astype(BF)
        first = jnp.concatenate([halo[0:LANES, at], products[:LANES]], axis=0)
        window = jnp.concatenate([first, products], axis=1)
        picked = pick_groups(
            jnp.dot(fwd_band[...], window, preferred_element_type=F32), per_tile, width
        )
        conv[0:LANES, at] = picked[:, :LANES]
        conv[LANES : 2 * LANES, at] = picked[:, LANES:]
        return carry

    lax.fori_loop(0, feats.shape[2] // LANES, tile, 0)


def forward_part(feats, taps, filters, halo):
    _, rows, channels = feats.shape
    groups = filters.shape[0]
    full = jax.ShapeDtypeStruct((rows, channels), F32)
    per_tile = groups * LANES // channels
    return pl.pallas_call(
        forward_kernel,
        out_shape=[full] * 4 + [jax.ShapeDtypeStruct((groups, LANES, 2 * LANES), BF)],
        in_specs=vmem(4),
        out_specs=vmem(5),
        scratch_shapes=[
            pltpu.VMEM((per_tile * LANES, 2 * LANES), BF),
            pltpu.VMEM((groups, LANES), F32),
            pltpu.VMEM((groups, LANES), F32),
            pltpu.VMEM((rows + 8, LANES), F32),
        ],
        compiler_params=params(20),
        cost_estimate=pl.CostEstimate(flops=2 << 30, bytes_accessed=12 << 20, transcendentals=0),
        name="forward_part",
    )(feats, taps, filters, halo)


def gate_kernel(keep0, keep1, got0, got1, last0, last1, conv, gate, feats, grad_conv, grad_gate, halo):
    cols = keep0.shape[2]
    for half, (keep, got, last) in enumerate(((keep0, got0, last0), (keep1, got1, last1))):
        at = slice(half * cols, (half + 1) * cols)
        grad_y = (keep[0] + got[0].astype(F32)) + last[...].astype(F32)
        grad_y = grad_y.astype(BF).astype(F32)
        down = (grad_y * gate[:, at]).astype(BF)
        across = (grad_y * conv[:, at]).astype(BF)
        grad_conv[:, at] = down
        grad_gate[:, at] = across
        halo[0:LANES, at] = down[:LANES]
        pieces = [
            down[LANES : LANES + 16].astype(F32)[0:1],
            across[0:16].astype(F32)[0:2],
            feats[1, 0:16, at].astype(F32)[0:2],
            feats[2, 0:16, at].astype(F32)[0:2],
            jnp.zeros((9, cols), F32),
        ]
        halo[LANES:HALO, at] = jnp.concatenate(pieces, axis=0).astype(BF)


def gate_part(keep0, keep1, got0, got1, last0, last1, conv, gate, feats):
    rows, channels = conv.shape
    full = jax.ShapeDtypeStruct((rows, channels), BF)
    return pl.pallas_call(
        gate_kernel,
        out_shape=[full, full, jax.ShapeDtypeStruct((HALO, channels), BF)],
        in_specs=vmem(9),
        out_specs=vmem(3),
        compiler_params=params(16),
        cost_estimate=pl.CostEstimate(flops=1 << 20, bytes_accessed=6 << 20, transcendentals=0),
        name="gate_part",
    )(keep0, keep1, got0, got1, last0, last1, conv, gate, feats)


def final_kernel(grad_conv, grad_gate, halo, key, value, feats, taps, back, out, ext, small):
    rows = grad_conv.shape[0]
    groups = back.shape[0]
    per_tile = groups * LANES // grad_conv.shape[1]
    width = LANES // per_tile

    def tile(l, carry):
        at = lane_tile(l)
        mine = grad_conv[:, at]
        after = halo[0:LANES, at]
        second = jnp.concatenate([mine[LANES:], after], axis=0)
        window = jnp.concatenate([mine, second], axis=1)
        first_group = pl.multiple_of(l * per_tile, per_tile)
        band = back[pl.ds(first_group, per_tile)]
        picked = pick_groups(
            jnp.dot(
                band.reshape(per_tile * LANES, 2 * LANES), window, preferred_element_type=F32
            ),
            per_tile,
            width,
        )
        rim = halo[LANES:HALO, at]
        beyond = jnp.concatenate([after, rim, jnp.zeros((LANES - 16, LANES), BF)], axis=0)
        top = band[:, 0:16, :].reshape(per_tile * 16, 2 * LANES)
        extra = pick_groups(jnp.dot(top, beyond, preferred_element_type=F32), per_tile, width)[0:2]
        rim_f = rim.astype(F32)
        streams = []
        for i, stream in ((1, value), (2, key)):
            other = 3 - i
            small[0:8] = feats[other, rows - 16 : rows, at].astype(F32)[8:16]
            small[8:16] = jnp.concatenate(
                [rim_f[1 + 2 * other : 3 + 2 * other], jnp.zeros((6, LANES), F32)], axis=0
            )
            beyond_mixed = (
                taps[other : other + 1, at] * small[8:10]
                + taps[3 + other : 4 + other, at] * small[7:9]
                + taps[6 + other : 7 + other, at] * small[6:8]
            )
            streams.append((i, stream, (extra * beyond_mixed).astype(BF).astype(F32)))

        def finish(i, mix_beyond):
            ext[rows : rows + 8] = jnp.concatenate([mix_beyond, jnp.zeros((6, LANES), F32)], axis=0)
            result = (
                taps[i : i + 1, at] * ext[0:rows]
                + taps[3 + i : 4 + i, at] * ext[1 : rows + 1]
                + taps[6 + i : 7 + i, at] * ext[2 : rows + 2]
            )
            out[i, :, at] = result.astype(BF)

        ext[0:rows] = grad_gate[:, at].astype(F32)
        finish(0, rim_f[1:3])
        for i, stream, mix_beyond in streams:
            ext[0:LANES] = (picked[:, :LANES] * stream[0:LANES, at]).astype(BF).astype(F32)
            ext[LANES : 2 * LANES] = (
                (picked[:, LANES:] * stream[LANES : 2 * LANES, at]).astype(BF).astype(F32)
            )
            finish(i, mix_beyond)
        return carry

    lax.fori_loop(0, grad_conv.shape[1] // LANES, tile, 0)


def final_part(grad_conv, grad_gate, halo, key, value, feats, taps, back):
    rows, channels = grad_conv.shape
    return pl.pallas_call(
        final_kernel,
        out_shape=jax.ShapeDtypeStruct((3, rows, channels), BF),
        in_specs=vmem(8),
        out_specs=vmem(1)[0],
        scratch_shapes=[pltpu.VMEM((rows + 8, LANES), F32), pltpu.VMEM((16, LANES), F32)],
        compiler_params=params(20),
        cost_estimate=pl.CostEstimate(flops=2 << 30, bytes_accessed=12 << 20, transcendentals=0),
        name="final_part",
    )(grad_conv, grad_gate, halo, key, value, feats, taps, back)


def local(features, short_taps, long_filters, out_weight, out_grad):
    feats = jnp.transpose(features[0], (1, 0, 2))
    rows, channels = feats.shape[1:]
    taps = short_taps[0].reshape(9, channels)
    filters = jnp.transpose(long_filters[0])
    weight = out_weight[0]
    cotangent = out_grad[0]

    half = channels // 2
    b_held = gather_halves((weight[:half], weight[half:]), pair_z)
    quarters = jnp.transpose(cotangent.reshape(rows, X, LANES), (1, 0, 2))
    along_x = [[z * X + x for x in range(X)] for z in range(RING)]
    block = lax.all_to_all(quarters, "ctx", 0, 0, axis_index_groups=along_x)
    block = block.reshape(X * rows, LANES)
    a_held = gather_halves((block[: X * rows // 2], block[X * rows // 2 :]), pair_tp)

    halo_before = shift_ctx(tail_rows(feats, taps), 1)
    conv, gate, key, value, back = forward_part(feats, taps, filters, halo_before)

    send0, send1, keep0, keep1 = partial_products(a_held, b_held)
    got0 = pair_x(send0, 1)
    got1 = pair_x(send1, 3)
    last0 = pair_x((keep0[1] + got0[1].astype(F32)).astype(BF), 3)
    last1 = pair_x((keep1[1] + got1[1].astype(F32)).astype(BF), 1)
    grad_conv, grad_gate, halo = gate_part(
        keep0, keep1, got0, got1, last0, last1, conv, gate, feats
    )
    halo_after = shift_ctx(halo, -1)
    grad_feat = final_part(grad_conv, grad_gate, halo_after, key, value, feats, taps, back)
    passed = lax.ppermute(grad_feat, "pp", [(0, 1), (1, 0)])
    return jnp.transpose(passed, (1, 0, 2))[None]


def solution(mesh):
    in_specs = (
        P("pp", "ctx", None, "tp"),
        P("pp", None, None, "tp"),
        P("pp", None, "tp"),
        P("pp", "tp", "ctx"),
        P("pp", "ctx", "tp"),
    )
    out_specs = P("pp", "ctx", None, "tp")
    return jax.shard_map(local, mesh=mesh, in_specs=in_specs, out_specs=out_specs, check_vma=False)
```

```python
import jax
import jax.numpy as jnp
from jax import lax
from jax.experimental import pallas as pl
from jax.experimental.pallas import tpu as pltpu
from jax.sharding import PartitionSpec as P

BF = jnp.bfloat16
F32 = jnp.float32
LANES = 128
X = 4
RING = 8
HALO = 144
HEAD = 144


def vmem(n):
    return [pl.BlockSpec(memory_space=pltpu.VMEM)] * n


def params(mib):
    return pltpu.CompilerParams(vmem_limit_bytes=mib << 20)


def partner(i, parity):
    return (i + 1) % RING if i % 2 == parity else (i - 1) % RING


def pair_ring(v, axis, turn):
    route = []
    for i in range(RING):
        for p in range(2):
            route.append((i * 2 + p, partner(i, (p + turn) % 2) * 2 + p))
    return lax.ppermute(v, (axis, "pp"), route)


def pair_x(v, flips):
    route = [(x * 2 + p, (x ^ flips[p]) * 2 + p) for x in range(X) for p in range(2)]
    return lax.ppermute(v, ("x", "pp"), route)


def swap(v):
    return lax.ppermute(v, "pp", [(0, 1), (1, 0)])


def shift_ctx(v, by, cross):
    n = RING * X
    route = []
    for i in range(n):
        for p in range(2):
            if 0 <= i + by < n:
                route.append((i * 2 + p, (i + by) * 2 + (p ^ cross)))
    return lax.ppermute(v, ("z", "x", "pp"), route)


def gather_ring(own, axis):
    first = pair_ring(own, axis, 0)
    pair = jnp.stack([own, first])
    second = pair_ring(pair, axis, 1)
    third = pair_ring(second, axis, 0)
    fourth = pair_ring(third, axis, 1)
    return [pair, second, third, fourth]


def offsets(step):
    return [(0, step), (-step, -2 * step), (2 * step, 3 * step), (-3 * step, -4 * step)]


def place(held, early, late, base, full_ref, me, core, pieces):
    rows = full_ref.shape[0] // (2 * pieces)
    mine = jnp.where(lax.rem(me, 2) == core, 1, -1)
    other = 1 - core

    def put(value, half, index):
        at = pl.multiple_of(lax.rem(index + 2 * RING, RING) * LANES, LANES)
        for n in range(pieces):
            top = pl.multiple_of(half * rows + 2 * n * rows, rows)
            full_ref[pl.ds(top, rows), pl.ds(at, LANES)] = value[n * rows : (n + 1) * rows]

    for n, pairs in enumerate(offsets(mine)):
        for k in range(2):
            put(held[n][k, other], core, me + pairs[k])
    for n, pairs in enumerate(offsets(-mine)):
        for k in range(2):
            value = early[base * 6 + 2 * n + k] if n < 3 else late[base * 2 + k]
            put(value, other, me + pairs[k])


def trade_kernel(*refs):
    out = refs[-1]
    core = lax.axis_index("pp")
    for n, ref in enumerate(refs[:-1]):
        for k in range(2):
            out[2 * n + k] = ref[k, core]


def trade(blocks):
    count = 2 * len(blocks)
    _, _, rows, lanes = blocks[0].shape
    picked = pl.pallas_call(
        trade_kernel,
        out_shape=jax.ShapeDtypeStruct((count, rows, lanes), BF),
        in_specs=vmem(len(blocks)),
        out_specs=vmem(1)[0],
        compiler_params=params(4),
        cost_estimate=pl.CostEstimate(flops=1 << 10, bytes_accessed=count << 18, transcendentals=0),
        name="trade",
    )(*blocks)
    return swap(picked)


def block_product(a_full, b_full, dest, tail):
    rows = a_full.shape[0] // X
    at = pl.multiple_of(dest * rows + (HEAD if tail else 0), 16)
    return lax.dot_general(
        a_full[pl.ds(at, rows - HEAD if tail else HEAD), :],
        b_full[...],
        (((1,), (1,)), ((), ())),
        preferred_element_type=F32,
    )


def flips_of(core):
    x = lax.axis_index("x")
    near = x + 1 - 2 * lax.rem(x, 2)
    far = 3 - x
    first = jnp.where(core == 0, near, far)
    second = jnp.where(core == 0, far, near)
    return x, first, second, 3 - near


def assemble_kernel(*refs):
    a_held, b_held, (early, late), (a_full, b_full, send) = refs[:4], refs[4:8], refs[8:10], refs[10:]
    core = lax.axis_index("pp")
    place(a_held, early, late, 0, a_full, lax.axis_index("tp"), core, X)
    place(b_held, early, late, 1, b_full, lax.axis_index("z"), core, 1)
    x, first, second, across = flips_of(core)
    send[0] = block_product(a_full, b_full, first, 0).astype(BF)
    send[1] = block_product(a_full, b_full, across, 0).astype(BF)


def remaining_kernel(a_full, b_full, send_tail, keep_head, keep_tail):
    core = lax.axis_index("pp")
    x, first, second, across = flips_of(core)
    send_tail[0] = block_product(a_full, b_full, second, 1).astype(BF)
    send_tail[1] = block_product(a_full, b_full, across, 1).astype(BF)
    keep_head[0] = block_product(a_full, b_full, x, 0)
    keep_head[1] = block_product(a_full, b_full, second, 0)
    keep_tail[0] = block_product(a_full, b_full, x, 1)
    keep_tail[1] = block_product(a_full, b_full, first, 1)


def partial_products(a_held, b_held, early, late):
    rows = 2 * a_held[0].shape[2]
    cols = 2 * b_held[0].shape[2]
    depth = RING * LANES
    head = (2, HEAD, cols)
    tail = (2, rows // X - HEAD, cols)
    a_full, b_full, send_head = pl.pallas_call(
        assemble_kernel,
        out_shape=[
            jax.ShapeDtypeStruct((rows, depth), BF),
            jax.ShapeDtypeStruct((cols, depth), BF),
            jax.ShapeDtypeStruct(head, BF),
        ],
        in_specs=vmem(10),
        out_specs=vmem(3),
        compiler_params=params(8),
        cost_estimate=pl.CostEstimate(flops=1 << 29, bytes_accessed=8 << 20, transcendentals=0),
        name="assemble",
    )(*a_held, *b_held, early, late)
    send_tail, keep_head, keep_tail = pl.pallas_call(
        remaining_kernel,
        out_shape=[
            jax.ShapeDtypeStruct(tail, BF),
            jax.ShapeDtypeStruct(head, F32),
            jax.ShapeDtypeStruct(tail, F32),
        ],
        in_specs=vmem(2),
        out_specs=vmem(3),
        compiler_params=params(8),
        cost_estimate=pl.CostEstimate(flops=3 << 29, bytes_accessed=8 << 20, transcendentals=0),
        name="remaining",
    )(a_full, b_full)
    return send_head, send_tail, keep_head, keep_tail


def fold_kernel(keep, got, out):
    out[...] = (keep[1] + got[1].astype(F32)).astype(BF)


def fold(keep, got):
    return pl.pallas_call(
        fold_kernel,
        out_shape=jax.ShapeDtypeStruct(got.shape[1:], BF),
        in_specs=vmem(2),
        out_specs=vmem(1)[0],
        compiler_params=params(4),
        cost_estimate=pl.CostEstimate(flops=1 << 17, bytes_accessed=1 << 20, transcendentals=0),
        name="fold",
    )(keep, got)


def quarter_kernel(cotangent, out):
    rows = cotangent.shape[0] // 2
    for p in range(2):
        for x in range(X):
            out[p * X + x] = cotangent[p * rows : (p + 1) * rows, x * LANES : (x + 1) * LANES]


def quarters_of(cotangent):
    return pl.pallas_call(
        quarter_kernel,
        out_shape=jax.ShapeDtypeStruct((2 * X, cotangent.shape[0] // 2, LANES), BF),
        in_specs=vmem(1),
        out_specs=vmem(1)[0],
        compiler_params=params(4),
        cost_estimate=pl.CostEstimate(flops=1 << 10, bytes_accessed=1 << 19, transcendentals=0),
        name="quarters",
    )(cotangent)


def lane_tile(index):
    return pl.ds(pl.multiple_of(index * LANES, LANES), LANES)


def tail_kernel(feats, taps, out, ext):
    rows = feats.shape[1]
    keep = rows - LANES

    def tile(l, carry):
        at = lane_tile(l)
        mixed = []
        for i in (1, 2):
            ext[...] = feats[i, keep - 16 : rows, at].astype(F32)
            mixed.append(
                taps[i : i + 1, at] * ext[16 : 16 + LANES]
                + taps[3 + i : 4 + i, at] * ext[15 : 15 + LANES]
                + taps[6 + i : 7 + i, at] * ext[14 : 14 + LANES]
            )
        out[0:LANES, at] = (mixed[0] * mixed[1]).astype(BF)
        last = [feats[i, rows - 16 : rows, at].astype(F32)[14:16] for i in range(3)]
        last.append(jnp.zeros((10, LANES), F32))
        out[LANES:HALO, at] = jnp.concatenate(last, axis=0).astype(BF)
        return carry

    lax.fori_loop(0, feats.shape[2] // LANES, tile, 0)


def tail_rows(feats, taps):
    channels = feats.shape[2]
    return pl.pallas_call(
        tail_kernel,
        out_shape=jax.ShapeDtypeStruct((HALO, channels), BF),
        in_specs=vmem(2),
        out_specs=vmem(1)[0],
        scratch_shapes=[pltpu.VMEM((LANES + 16, LANES), F32)],
        compiler_params=params(8),
        cost_estimate=pl.CostEstimate(flops=1 << 20, bytes_accessed=2 << 20, transcendentals=0),
        name="tail_rows",
    )(feats, taps)


def pick_groups(product, per_tile, width):
    rows = product.shape[0] // per_tile
    shape = (rows, product.shape[1])
    group = lax.rem(lax.broadcasted_iota(jnp.int32, shape, 1), LANES) // width
    out = product[:rows]
    for g in range(1, per_tile):
        out = jnp.where(group == g, product[g * rows : (g + 1) * rows], out)
    return out


def forward_kernel(feats, taps, filters, halo, conv, gate, key, value, back, fwd_band, flipped, plain, ext):
    rows = feats.shape[1]
    groups = filters.shape[0]
    per_tile = groups * LANES // feats.shape[2]
    width = LANES // per_tile
    row = lax.broadcasted_iota(jnp.int32, (LANES, LANES), 0)
    col = lax.broadcasted_iota(jnp.int32, (LANES, LANES), 1)
    mirror = jnp.where(lax.rem(row + col, LANES) == 0, 1.0, 0.0).astype(BF)
    flipped[...] = jnp.dot(filters[...], mirror, preferred_element_type=F32)
    plain[...] = filters[...].astype(F32)

    def tile(l, carry):
        at = lane_tile(l)
        for g in range(per_tile):
            index = l * per_tile + g
            spread = jnp.broadcast_to(plain[pl.ds(index, 1), :], (LANES, LANES))
            turned = pltpu.roll(spread, 0, 1, stride=1, stride_axis=0)
            back[index, :, 0:LANES] = jnp.where(col >= row, turned, 0.0).astype(BF)
            back[index, :, LANES : 2 * LANES] = jnp.where(col < row, turned, 0.0).astype(BF)
            spread = jnp.broadcast_to(flipped[pl.ds(index, 1), :], (LANES, LANES))
            turned = pltpu.roll(spread, 0, 1, stride=1, stride_axis=0)
            fwd_band[g * LANES : (g + 1) * LANES, 0:LANES] = jnp.where(col > row, turned, 0.0).astype(BF)
            fwd_band[g * LANES : (g + 1) * LANES, LANES : 2 * LANES] = jnp.where(
                col <= row, turned, 0.0
            ).astype(BF)
        before = halo[LANES:HALO, at].astype(F32)
        mixed = []
        for i in range(3):
            ext[0:8] = jnp.concatenate([jnp.zeros((6, LANES), F32), before[2 * i : 2 * i + 2]], axis=0)
            ext[8 : 8 + rows] = feats[i, :, at].astype(F32)
            mixed.append(
                taps[i : i + 1, at] * ext[8 : 8 + rows]
                + taps[3 + i : 4 + i, at] * ext[7 : 7 + rows]
                + taps[6 + i : 7 + i, at] * ext[6 : 6 + rows]
            )
        gate[:, at] = mixed[0]
        key[:, at] = mixed[1]
        value[:, at] = mixed[2]
        products = (mixed[1] * mixed[2]).astype(BF)
        first = jnp.concatenate([halo[0:LANES, at], products[:LANES]], axis=0)
        window = jnp.concatenate([first, products], axis=1)
        picked = pick_groups(
            jnp.dot(fwd_band[...], window, preferred_element_type=F32), per_tile, width
        )
        conv[0:LANES, at] = picked[:, :LANES]
        conv[LANES : 2 * LANES, at] = picked[:, LANES:]
        return carry

    lax.fori_loop(0, feats.shape[2] // LANES, tile, 0)


def forward_part(feats, taps, filters, halo):
    _, rows, channels = feats.shape
    groups = filters.shape[0]
    full = jax.ShapeDtypeStruct((rows, channels), F32)
    per_tile = groups * LANES // channels
    return pl.pallas_call(
        forward_kernel,
        out_shape=[full] * 4 + [jax.ShapeDtypeStruct((groups, LANES, 2 * LANES), BF)],
        in_specs=vmem(4),
        out_specs=vmem(5),
        scratch_shapes=[
            pltpu.VMEM((per_tile * LANES, 2 * LANES), BF),
            pltpu.VMEM((groups, LANES), F32),
            pltpu.VMEM((groups, LANES), F32),
            pltpu.VMEM((rows + 8, LANES), F32),
        ],
        compiler_params=params(20),
        cost_estimate=pl.CostEstimate(flops=2 << 30, bytes_accessed=12 << 20, transcendentals=0),
        name="forward_part",
    )(feats, taps, filters, halo)


def gated(keep, got, last, conv, gate, grad_conv, grad_gate):
    grad_y = (keep[0] + got[0].astype(F32)) + last[...].astype(F32)
    grad_y = grad_y.astype(BF).astype(F32)
    down = (grad_y * gate).astype(BF)
    across = (grad_y * conv).astype(BF)
    grad_conv[...] = down
    grad_gate[...] = across
    return down, across


def head_kernel(keep, got, last, conv, gate, feats, grad_conv, grad_gate, halo):
    down, across = gated(keep, got, last, conv[0:HEAD], gate[0:HEAD], grad_conv, grad_gate)
    halo[0:LANES] = down[0:LANES]
    pieces = [
        down[LANES:HEAD].astype(F32)[0:1],
        across[0:16].astype(F32)[0:2],
        feats[1, 0:16].astype(F32)[0:2],
        feats[2, 0:16].astype(F32)[0:2],
        jnp.zeros((9, down.shape[1]), F32),
    ]
    halo[LANES:HALO] = jnp.concatenate(pieces, axis=0).astype(BF)


def tail_gate_kernel(keep, got, last, conv, gate, grad_conv, grad_gate):
    rows = conv.shape[0]
    gated(keep, got, last, conv[HEAD:rows], gate[HEAD:rows], grad_conv, grad_gate)


def gate_head(keep, got, last, conv, gate, feats):
    half = jax.ShapeDtypeStruct(last.shape, BF)
    return pl.pallas_call(
        head_kernel,
        out_shape=[half, half, jax.ShapeDtypeStruct((HALO, last.shape[1]), BF)],
        in_specs=vmem(6),
        out_specs=vmem(3),
        compiler_params=params(8),
        cost_estimate=pl.CostEstimate(flops=1 << 20, bytes_accessed=3 << 20, transcendentals=0),
        name="gate_head",
    )(keep, got, last, conv, gate, feats)


def gate_tail(keep, got, last, conv, gate):
    half = jax.ShapeDtypeStruct(last.shape, BF)
    return pl.pallas_call(
        tail_gate_kernel,
        out_shape=[half, half],
        in_specs=vmem(5),
        out_specs=vmem(2),
        compiler_params=params(8),
        cost_estimate=pl.CostEstimate(flops=1 << 20, bytes_accessed=3 << 20, transcendentals=0),
        name="gate_tail",
    )(keep, got, last, conv, gate)


def final_kernel(
    conv_head, conv_tail, gate_head, gate_tail, halo, key, value, feats, taps, back, out, ext, small
):
    rows = key.shape[0]
    groups = back.shape[0]
    per_tile = groups * LANES // key.shape[1]
    width = LANES // per_tile

    def tile(l, carry):
        at = lane_tile(l)
        mine = jnp.concatenate([conv_head[:, at], conv_tail[:, at]], axis=0)
        after = halo[0:LANES, at]
        second = jnp.concatenate([mine[LANES:], after], axis=0)
        window = jnp.concatenate([mine, second], axis=1)
        first_group = pl.multiple_of(l * per_tile, per_tile)
        band = back[pl.ds(first_group, per_tile)]
        picked = pick_groups(
            jnp.dot(
                band.reshape(per_tile * LANES, 2 * LANES), window, preferred_element_type=F32
            ),
            per_tile,
            width,
        )
        rim = halo[LANES:HALO, at]
        beyond = jnp.concatenate([after, rim, jnp.zeros((LANES - 16, LANES), BF)], axis=0)
        top = band[:, 0:16, :].reshape(per_tile * 16, 2 * LANES)
        extra = pick_groups(jnp.dot(top, beyond, preferred_element_type=F32), per_tile, width)[0:2]
        rim_f = rim.astype(F32)
        streams = []
        for i, stream in ((1, value), (2, key)):
            other = 3 - i
            small[0:8] = feats[other, rows - 16 : rows, at].astype(F32)[8:16]
            small[8:16] = jnp.concatenate(
                [rim_f[1 + 2 * other : 3 + 2 * other], jnp.zeros((6, LANES), F32)], axis=0
            )
            beyond_mixed = (
                taps[other : other + 1, at] * small[8:10]
                + taps[3 + other : 4 + other, at] * small[7:9]
                + taps[6 + other : 7 + other, at] * small[6:8]
            )
            streams.append((i, stream, (extra * beyond_mixed).astype(BF).astype(F32)))

        def finish(i, mix_beyond):
            ext[rows : rows + 8] = jnp.concatenate([mix_beyond, jnp.zeros((6, LANES), F32)], axis=0)
            result = (
                taps[i : i + 1, at] * ext[0:rows]
                + taps[3 + i : 4 + i, at] * ext[1 : rows + 1]
                + taps[6 + i : 7 + i, at] * ext[2 : rows + 2]
            )
            out[i, :, at] = result.astype(BF)

        ext[0:HEAD] = gate_head[:, at].astype(F32)
        ext[HEAD:rows] = gate_tail[:, at].astype(F32)
        finish(0, rim_f[1:3])
        for i, stream, mix_beyond in streams:
            ext[0:LANES] = (picked[:, :LANES] * stream[0:LANES, at]).astype(BF).astype(F32)
            ext[LANES : 2 * LANES] = (
                (picked[:, LANES:] * stream[LANES : 2 * LANES, at]).astype(BF).astype(F32)
            )
            finish(i, mix_beyond)
        return carry

    lax.fori_loop(0, key.shape[1] // LANES, tile, 0)


def final_part(convs, gates, halo, key, value, feats, taps, back):
    rows, channels = key.shape
    return pl.pallas_call(
        final_kernel,
        out_shape=jax.ShapeDtypeStruct((3, rows, channels), BF),
        in_specs=vmem(10),
        out_specs=vmem(1)[0],
        scratch_shapes=[pltpu.VMEM((rows + 8, LANES), F32), pltpu.VMEM((16, LANES), F32)],
        compiler_params=params(20),
        cost_estimate=pl.CostEstimate(flops=2 << 30, bytes_accessed=12 << 20, transcendentals=0),
        name="final_part",
    )(*convs, *gates, halo, key, value, feats, taps, back)


def local(features, short_taps, long_filters, out_weight, out_grad):
    feats = jnp.transpose(features[0], (1, 0, 2))
    rows, channels = feats.shape[1:]
    taps = short_taps[0].reshape(9, channels)
    filters = jnp.transpose(long_filters[0])

    halves = out_weight[0].reshape(2, channels // 2, LANES)
    b_own = lax.all_to_all(halves, "pp", 0, 0)
    a_own = lax.all_to_all(quarters_of(out_grad[0]), ("pp", "x"), 0, 0)
    a_own = a_own.reshape(2, X * rows // 2, LANES)
    b_held = gather_ring(b_own, "z")
    a_held = gather_ring(a_own, "tp")
    early = trade(a_held[:3] + b_held[:3])
    late = trade([a_held[3], b_held[3]])

    halo_before = shift_ctx(tail_rows(feats, taps), 1, 1)
    feats = swap(feats)
    taps = lax.ppermute(short_taps[0], "pp", [(0, 1), (1, 0)]).reshape(9, channels)
    filters = swap(filters)
    conv, gate, key, value, back = forward_part(feats, taps, filters, halo_before)

    send_head, send_tail, keep_head, keep_tail = partial_products(a_held, b_held, early, late)
    got_head = pair_x(send_head, (1, 3))
    got_tail = pair_x(send_tail, (3, 1))
    last_head = pair_x(fold(keep_head, got_head), (3, 1))
    last_tail = pair_x(fold(keep_tail, got_tail), (1, 3))
    conv_head, cross_head, halo = gate_head(keep_head, got_head, last_head, conv, gate, feats)
    conv_tail, cross_tail = gate_tail(keep_tail, got_tail, last_tail, conv, gate)
    halo_after = shift_ctx(halo, -1, 0)
    grad_feat = final_part(
        (conv_head, conv_tail), (cross_head, cross_tail), halo_after, key, value, feats, taps, back
    )
    return jnp.transpose(grad_feat, (1, 0, 2))[None]


def solution(mesh):
    parts = jax.sharding.Mesh(
        mesh.devices.reshape(RING, X, RING, 2),
        ("z", "x", "tp", "pp"),
        axis_types=(jax.sharding.AxisType.Auto,) * 4,
    )
    ctx = ("z", "x")
    in_specs = (
        P("pp", ctx, None, "tp"),
        P("pp", None, None, "tp"),
        P("pp", None, "tp"),
        P("pp", "tp", ctx),
        P("pp", ctx, "tp"),
    )
    out_specs = P("pp", ctx, None, "tp")
    return jax.shard_map(local, mesh=parts, in_specs=in_specs, out_specs=out_specs, check_vma=False)
```

```python
import jax
import jax.numpy as jnp
from jax import lax
from jax.experimental import pallas as pl
from jax.experimental.pallas import tpu as pltpu
from jax.sharding import PartitionSpec as P

BF = jnp.bfloat16
F32 = jnp.float32
LANES = 128
X = 4
RING = 8
HALO = 144
HEAD = 144


def vmem(n):
    return [pl.BlockSpec(memory_space=pltpu.VMEM)] * n


def params(mib):
    return pltpu.CompilerParams(vmem_limit_bytes=mib << 20)


def partner(i, parity):
    return (i + 1) % RING if i % 2 == parity else (i - 1) % RING


def pair_ring(v, axis, parity):
    return lax.ppermute(v, axis, [(i, partner(i, parity)) for i in range(RING)])


def pair_x(v, flip, cross):
    route = [(x * 2 + p, (x ^ flip) * 2 + (p ^ cross)) for x in range(X) for p in range(2)]
    return lax.ppermute(v, ("x", "pp"), route)


def swap(v):
    return lax.ppermute(v, "pp", [(0, 1), (1, 0)])


def shift_ctx(v, by, cross):
    n = RING * X
    route = []
    for i in range(n):
        for p in range(2):
            if 0 <= i + by < n:
                route.append((i * 2 + p, (i + by) * 2 + (p ^ cross)))
    return lax.ppermute(v, ("z", "x", "pp"), route)


def join_kernel(own, first, out):
    out[0] = own[...]
    out[1] = first[...]


def join(own, first):
    return pl.pallas_call(
        join_kernel,
        out_shape=jax.ShapeDtypeStruct((2,) + own.shape, BF),
        in_specs=vmem(2),
        out_specs=vmem(1)[0],
        compiler_params=params(2),
        cost_estimate=pl.CostEstimate(flops=1 << 10, bytes_accessed=1 << 18, transcendentals=0),
        name="join",
    )(own, first)


def gather_ring(halves, axis):
    def hop(n, turn, v):
        return pair_ring(v, axis, (n + turn) % 2)

    firsts = [hop(n, 0, halves[n]) for n in range(2)]
    held = [[join(halves[n], firsts[n]) for n in range(2)]]
    for turn in (1, 2, 3):
        now = lax.optimization_barrier(held[-1])
        held.append([hop(n, turn, now[n]) for n in range(2)])
    return held


def place(held, full_ref, me, flip):
    rows = full_ref.shape[0] // 2
    pieces = 1 if flip is None else X // 2
    size = rows // pieces
    for n in range(2):
        step = jnp.where(lax.rem(me, 2) == n, 1, -1)
        spots = [(0, step), (-step, -2 * step), (2 * step, 3 * step), (-3 * step, -4 * step)]
        for turn in range(4):
            for k in range(2):
                index = lax.rem(me + spots[turn][k] + 2 * RING, RING)
                at = pl.multiple_of(index * LANES, LANES)
                for m in range(pieces):
                    slot = n if flip is None else jnp.bitwise_xor(n * pieces + m, flip)
                    top = pl.multiple_of(slot * size, size)
                    full_ref[pl.ds(top, size), pl.ds(at, LANES)] = held[turn * 2 + n][
                        k, m * size : (m + 1) * size
                    ]


def matmul_kernel(*refs):
    a_held, b_held, outs, (a_full, b_full) = refs[:8], refs[8:16], refs[16:20], refs[20:]
    send_head, send_tail, keep_head, keep_tail = outs
    place(a_held, a_full, lax.axis_index("tp"), lax.axis_index("x"))
    place(b_held, b_full, lax.axis_index("z"), None)
    rows = a_full.shape[0] // X
    width = 2 * LANES

    def columns(c, carry):
        at = pl.multiple_of(c * width, width)
        product = lax.dot_general(
            a_full[...],
            b_full[pl.ds(at, width), :],
            (((1,), (1,)), ((), ())),
            preferred_element_type=F32,
        )
        own, near, across, far = [product[n * rows : (n + 1) * rows] for n in range(X)]
        here = pl.ds(at, width)
        send_head[0, :, here] = near[:HEAD].astype(BF)
        send_head[1, :, here] = across[:HEAD].astype(BF)
        send_tail[0, :, here] = far[HEAD:].astype(BF)
        send_tail[1, :, here] = across[HEAD:].astype(BF)
        keep_head[0, :, here] = own[:HEAD]
        keep_head[1, :, here] = far[:HEAD]
        keep_tail[0, :, here] = own[HEAD:]
        keep_tail[1, :, here] = near[HEAD:]
        return carry

    lax.fori_loop(0, b_full.shape[0] // width, columns, 0)


def partial_products(a_held, b_held):
    a_list = [v for parts in a_held for v in parts]
    b_list = [v for parts in b_held for v in parts]
    rows = 2 * a_list[0].shape[1]
    cols = 2 * b_list[0].shape[1]
    depth = RING * LANES
    head = (2, HEAD, cols)
    tail = (2, rows // X - HEAD, cols)
    return pl.pallas_call(
        matmul_kernel,
        out_shape=[
            jax.ShapeDtypeStruct(head, BF),
            jax.ShapeDtypeStruct(tail, BF),
            jax.ShapeDtypeStruct(head, F32),
            jax.ShapeDtypeStruct(tail, F32),
        ],
        in_specs=vmem(16),
        out_specs=vmem(4),
        scratch_shapes=[pltpu.VMEM((rows, depth), BF), pltpu.VMEM((cols, depth), BF)],
        compiler_params=params(10),
        cost_estimate=pl.CostEstimate(
            flops=2 * rows * cols * depth, bytes_accessed=8 << 20, transcendentals=0
        ),
        name="partial_products",
    )(*a_list, *b_list)


def fold_kernel(keep_head, got_head, keep_tail, got_tail, out_head, out_tail, own):
    out_head[...] = (keep_head[1] + got_head[1].astype(F32)).astype(BF)
    out_tail[...] = (keep_tail[1] + got_tail[1].astype(F32)).astype(BF)
    own[0:HEAD] = (keep_head[0] + got_head[0].astype(F32)).astype(BF)
    own[HEAD:] = (keep_tail[0] + got_tail[0].astype(F32)).astype(BF)


def fold(keep_head, got_head, keep_tail, got_tail):
    head, tail = got_head.shape[1:], got_tail.shape[1:]
    return pl.pallas_call(
        fold_kernel,
        out_shape=[
            jax.ShapeDtypeStruct(head, BF),
            jax.ShapeDtypeStruct(tail, BF),
            jax.ShapeDtypeStruct((head[0] + tail[0], head[1]), BF),
        ],
        in_specs=vmem(4),
        out_specs=vmem(3),
        compiler_params=params(2),
        cost_estimate=pl.CostEstimate(flops=1 << 18, bytes_accessed=4 << 20, transcendentals=0),
        name="fold",
    )(keep_head, got_head, keep_tail, got_tail)


def quarter_kernel(cotangent, out):
    for x in range(X):
        out[x] = cotangent[:, x * LANES : (x + 1) * LANES]


def quarters_of(cotangent):
    return pl.pallas_call(
        quarter_kernel,
        out_shape=jax.ShapeDtypeStruct((X, cotangent.shape[0], LANES), BF),
        in_specs=vmem(1),
        out_specs=vmem(1)[0],
        compiler_params=params(2),
        cost_estimate=pl.CostEstimate(flops=1 << 10, bytes_accessed=1 << 19, transcendentals=0),
        name="quarters",
    )(cotangent)


def lane_tile(index):
    return pl.ds(pl.multiple_of(index * LANES, LANES), LANES)


def tail_kernel(feats, taps, out, ext):
    rows = feats.shape[1]
    keep = rows - LANES

    def tile(l, carry):
        at = lane_tile(l)
        mixed = []
        for i in (1, 2):
            ext[...] = feats[i, keep - 16 : rows, at].astype(F32)
            mixed.append(
                taps[i : i + 1, at] * ext[16 : 16 + LANES]
                + taps[3 + i : 4 + i, at] * ext[15 : 15 + LANES]
                + taps[6 + i : 7 + i, at] * ext[14 : 14 + LANES]
            )
        out[0:LANES, at] = (mixed[0] * mixed[1]).astype(BF)
        last = [feats[i, rows - 16 : rows, at].astype(F32)[14:16] for i in range(3)]
        last.append(jnp.zeros((10, LANES), F32))
        out[LANES:HALO, at] = jnp.concatenate(last, axis=0).astype(BF)
        return carry

    lax.fori_loop(0, feats.shape[2] // LANES, tile, 0)


def tail_rows(feats, taps):
    channels = feats.shape[2]
    return pl.pallas_call(
        tail_kernel,
        out_shape=jax.ShapeDtypeStruct((HALO, channels), BF),
        in_specs=vmem(2),
        out_specs=vmem(1)[0],
        scratch_shapes=[pltpu.VMEM((LANES + 16, LANES), F32)],
        compiler_params=params(8),
        cost_estimate=pl.CostEstimate(flops=1 << 20, bytes_accessed=2 << 20, transcendentals=0),
        name="tail_rows",
    )(feats, taps)


def pick_groups(product, per_tile, width):
    rows = product.shape[0] // per_tile
    shape = (rows, product.shape[1])
    group = lax.rem(lax.broadcasted_iota(jnp.int32, shape, 1), LANES) // width
    out = product[:rows]
    for g in range(1, per_tile):
        out = jnp.where(group == g, product[g * rows : (g + 1) * rows], out)
    return out


def forward_kernel(feats, taps, filters, halo, conv, gate, key, value, back, fwd_band, flipped, plain, ext):
    rows = feats.shape[1]
    groups = filters.shape[0]
    per_tile = groups * LANES // feats.shape[2]
    width = LANES // per_tile
    row = lax.broadcasted_iota(jnp.int32, (LANES, LANES), 0)
    col = lax.broadcasted_iota(jnp.int32, (LANES, LANES), 1)
    mirror = jnp.where(lax.rem(row + col, LANES) == 0, 1.0, 0.0).astype(BF)
    flipped[...] = jnp.dot(filters[...], mirror, preferred_element_type=F32)
    plain[...] = filters[...].astype(F32)

    def tile(l, carry):
        at = lane_tile(l)
        for g in range(per_tile):
            index = l * per_tile + g
            spread = jnp.broadcast_to(plain[pl.ds(index, 1), :], (LANES, LANES))
            turned = pltpu.roll(spread, 0, 1, stride=1, stride_axis=0)
            back[index, :, 0:LANES] = jnp.where(col >= row, turned, 0.0).astype(BF)
            back[index, :, LANES : 2 * LANES] = jnp.where(col < row, turned, 0.0).astype(BF)
            spread = jnp.broadcast_to(flipped[pl.ds(index, 1), :], (LANES, LANES))
            turned = pltpu.roll(spread, 0, 1, stride=1, stride_axis=0)
            fwd_band[g * LANES : (g + 1) * LANES, 0:LANES] = jnp.where(col > row, turned, 0.0).astype(BF)
            fwd_band[g * LANES : (g + 1) * LANES, LANES : 2 * LANES] = jnp.where(
                col <= row, turned, 0.0
            ).astype(BF)
        before = halo[LANES:HALO, at].astype(F32)
        mixed = []
        for i in range(3):
            ext[0:8] = jnp.concatenate([jnp.zeros((6, LANES), F32), before[2 * i : 2 * i + 2]], axis=0)
            ext[8 : 8 + rows] = feats[i, :, at].astype(F32)
            mixed.append(
                taps[i : i + 1, at] * ext[8 : 8 + rows]
                + taps[3 + i : 4 + i, at] * ext[7 : 7 + rows]
                + taps[6 + i : 7 + i, at] * ext[6 : 6 + rows]
            )
        gate[:, at] = mixed[0]
        key[:, at] = mixed[1]
        value[:, at] = mixed[2]
        products = (mixed[1] * mixed[2]).astype(BF)
        first = jnp.concatenate([halo[0:LANES, at], products[:LANES]], axis=0)
        window = jnp.concatenate([first, products], axis=1)
        picked = pick_groups(
            jnp.dot(fwd_band[...], window, preferred_element_type=F32), per_tile, width
        )
        conv[0:LANES, at] = picked[:, :LANES]
        conv[LANES : 2 * LANES, at] = picked[:, LANES:]
        return carry

    lax.fori_loop(0, feats.shape[2] // LANES, tile, 0)


def forward_part(feats, taps, filters, halo):
    _, rows, channels = feats.shape
    groups = filters.shape[0]
    full = jax.ShapeDtypeStruct((rows, channels), F32)
    per_tile = groups * LANES // channels
    return pl.pallas_call(
        forward_kernel,
        out_shape=[full] * 4 + [jax.ShapeDtypeStruct((groups, LANES, 2 * LANES), BF)],
        in_specs=vmem(4),
        out_specs=vmem(5),
        scratch_shapes=[
            pltpu.VMEM((per_tile * LANES, 2 * LANES), BF),
            pltpu.VMEM((groups, LANES), F32),
            pltpu.VMEM((groups, LANES), F32),
            pltpu.VMEM((rows + 8, LANES), F32),
        ],
        compiler_params=params(8),
        cost_estimate=pl.CostEstimate(flops=2 << 30, bytes_accessed=12 << 20, transcendentals=0),
        name="forward_part",
    )(feats, taps, filters, halo)


def gated(own, last, conv, gate, grad_conv, grad_gate):
    grad_y = (own.astype(F32) + last[...].astype(F32)).astype(BF).astype(F32)
    down = (grad_y * gate).astype(BF)
    across = (grad_y * conv).astype(BF)
    grad_conv[...] = down
    grad_gate[...] = across
    return down, across


def head_kernel(own, last, conv, gate, feats, grad_conv, grad_gate, halo):
    down, across = gated(own[0:HEAD], last, conv[0:HEAD], gate[0:HEAD], grad_conv, grad_gate)
    halo[0:LANES] = down[0:LANES]
    pieces = [
        down[LANES:HEAD].astype(F32)[0:1],
        across[0:16].astype(F32)[0:2],
        feats[1, 0:16].astype(F32)[0:2],
        feats[2, 0:16].astype(F32)[0:2],
        jnp.zeros((9, down.shape[1]), F32),
    ]
    halo[LANES:HALO] = jnp.concatenate(pieces, axis=0).astype(BF)


def tail_gate_kernel(own, last, conv, gate, grad_conv, grad_gate):
    rows = conv.shape[0]
    gated(own[HEAD:rows], last, conv[HEAD:rows], gate[HEAD:rows], grad_conv, grad_gate)


def gate_head(own, last, conv, gate, feats):
    half = jax.ShapeDtypeStruct(last.shape, BF)
    return pl.pallas_call(
        head_kernel,
        out_shape=[half, half, jax.ShapeDtypeStruct((HALO, last.shape[1]), BF)],
        in_specs=vmem(5),
        out_specs=vmem(3),
        compiler_params=params(8),
        cost_estimate=pl.CostEstimate(flops=1 << 20, bytes_accessed=3 << 20, transcendentals=0),
        name="gate_head",
    )(own, last, conv, gate, feats)


def gate_tail(own, last, conv, gate):
    half = jax.ShapeDtypeStruct(last.shape, BF)
    return pl.pallas_call(
        tail_gate_kernel,
        out_shape=[half, half],
        in_specs=vmem(4),
        out_specs=vmem(2),
        compiler_params=params(8),
        cost_estimate=pl.CostEstimate(flops=1 << 20, bytes_accessed=3 << 20, transcendentals=0),
        name="gate_tail",
    )(own, last, conv, gate)


def final_kernel(
    conv_head, conv_tail, gate_head, gate_tail, halo, key, value, feats, taps, back, out, ext, small
):
    rows = key.shape[0]
    groups = back.shape[0]
    per_tile = groups * LANES // key.shape[1]
    width = LANES // per_tile

    def tile(l, carry):
        at = lane_tile(l)
        mine = jnp.concatenate([conv_head[:, at], conv_tail[:, at]], axis=0)
        after = halo[0:LANES, at]
        second = jnp.concatenate([mine[LANES:], after], axis=0)
        window = jnp.concatenate([mine, second], axis=1)
        first_group = pl.multiple_of(l * per_tile, per_tile)
        band = back[pl.ds(first_group, per_tile)]
        picked = pick_groups(
            jnp.dot(
                band.reshape(per_tile * LANES, 2 * LANES), window, preferred_element_type=F32
            ),
            per_tile,
            width,
        )
        rim = halo[LANES:HALO, at]
        beyond = jnp.concatenate([after, rim, jnp.zeros((LANES - 16, LANES), BF)], axis=0)
        top = band[:, 0:16, :].reshape(per_tile * 16, 2 * LANES)
        extra = pick_groups(jnp.dot(top, beyond, preferred_element_type=F32), per_tile, width)[0:2]
        rim_f = rim.astype(F32)
        streams = []
        for i, stream in ((1, value), (2, key)):
            other = 3 - i
            small[0:8] = feats[other, rows - 16 : rows, at].astype(F32)[8:16]
            small[8:16] = jnp.concatenate(
                [rim_f[1 + 2 * other : 3 + 2 * other], jnp.zeros((6, LANES), F32)], axis=0
            )
            beyond_mixed = (
                taps[other : other + 1, at] * small[8:10]
                + taps[3 + other : 4 + other, at] * small[7:9]
                + taps[6 + other : 7 + other, at] * small[6:8]
            )
            streams.append((i, stream, (extra * beyond_mixed).astype(BF).astype(F32)))

        def finish(i, mix_beyond):
            ext[rows : rows + 8] = jnp.concatenate([mix_beyond, jnp.zeros((6, LANES), F32)], axis=0)
            result = (
                taps[i : i + 1, at] * ext[0:rows]
                + taps[3 + i : 4 + i, at] * ext[1 : rows + 1]
                + taps[6 + i : 7 + i, at] * ext[2 : rows + 2]
            )
            out[i, :, at] = result.astype(BF)

        ext[0:HEAD] = gate_head[:, at].astype(F32)
        ext[HEAD:rows] = gate_tail[:, at].astype(F32)
        finish(0, rim_f[1:3])
        for i, stream, mix_beyond in streams:
            ext[0:LANES] = (picked[:, :LANES] * stream[0:LANES, at]).astype(BF).astype(F32)
            ext[LANES : 2 * LANES] = (
                (picked[:, LANES:] * stream[LANES : 2 * LANES, at]).astype(BF).astype(F32)
            )
            finish(i, mix_beyond)
        return carry

    lax.fori_loop(0, key.shape[1] // LANES, tile, 0)


def final_part(convs, gates, halo, key, value, feats, taps, back):
    rows, channels = key.shape
    return pl.pallas_call(
        final_kernel,
        out_shape=jax.ShapeDtypeStruct((3, rows, channels), BF),
        in_specs=vmem(10),
        out_specs=vmem(1)[0],
        scratch_shapes=[pltpu.VMEM((rows + 8, LANES), F32), pltpu.VMEM((16, LANES), F32)],
        compiler_params=params(8),
        cost_estimate=pl.CostEstimate(flops=2 << 30, bytes_accessed=12 << 20, transcendentals=0),
        name="final_part",
    )(*convs, *gates, halo, key, value, feats, taps, back)


def after(value, *others):
    return lax.optimization_barrier((value,) + others)[0]


def trade_x(quarters):
    return lax.all_to_all(quarters, "x", 0, 0)


def local(features, short_taps, long_filters, out_weight, out_grad):
    feats = jnp.transpose(features[0], (1, 0, 2))
    rows, channels = feats.shape[1:]
    taps = short_taps[0].reshape(9, channels)
    filters = jnp.transpose(long_filters[0])

    quarters = quarters_of(out_grad[0])
    weight = after(out_weight[0], quarters)
    block = trade_x(quarters).reshape(X * rows, LANES)
    b_held = gather_ring([weight[: channels // 2], weight[channels // 2 :]], "z")
    a_held = gather_ring([block[: X * rows // 2], block[X * rows // 2 :]], "tp")
    halo_before = shift_ctx(tail_rows(feats, taps), 1, 1)
    feats = swap(feats)
    taps = swap(taps)
    filters = swap(filters)
    conv, gate, key, value, back = forward_part(feats, taps, filters, halo_before)

    send_head, send_tail, keep_head, keep_tail = partial_products(a_held, b_held)
    got_head = pair_x(send_head, 1, 0)
    got_tail = pair_x(send_tail, 3, 0)
    head, tail, own = fold(keep_head, got_head, keep_tail, got_tail)
    last_head = pair_x(head, 3, 1)
    last_tail = pair_x(tail, 1, 1)
    own = swap(own)
    conv_head, cross_head, halo = gate_head(own, last_head, conv, gate, feats)
    conv_tail, cross_tail = gate_tail(own, last_tail, conv, gate)
    halo_after = shift_ctx(halo, -1, 0)
    grad_feat = final_part(
        (conv_head, conv_tail), (cross_head, cross_tail), halo_after, key, value, feats, taps, back
    )
    return jnp.transpose(grad_feat, (1, 0, 2))[None]


def solution(mesh):
    parts = jax.sharding.Mesh(
        mesh.devices.reshape(RING, X, RING, 2),
        ("z", "x", "tp", "pp"),
        axis_types=(jax.sharding.AxisType.Auto,) * 4,
    )
    ctx = ("z", "x")
    in_specs = (
        P("pp", ctx, None, "tp"),
        P("pp", None, None, "tp"),
        P("pp", None, "tp"),
        P("pp", "tp", ctx),
        P("pp", ctx, "tp"),
    )
    out_specs = P("pp", ctx, None, "tp")

    return jax.shard_map(local, mesh=parts, in_specs=in_specs, out_specs=out_specs, check_vma=False)
```

```python
import jax
import jax.numpy as jnp
from jax import lax
from jax.experimental import pallas as pl
from jax.experimental.pallas import tpu as pltpu
from jax.sharding import PartitionSpec as P

BF = jnp.bfloat16
F32 = jnp.float32
LANES = 128
X = 4
RING = 8
HALO = 144
HEAD = 144


def vmem(n):
    return [pl.BlockSpec(memory_space=pltpu.VMEM)] * n


def params(mib):
    return pltpu.CompilerParams(vmem_limit_bytes=mib << 20)


def partner(i, parity):
    return (i + 1) % RING if i % 2 == parity else (i - 1) % RING


def pair_ring(v, axis, parity):
    return lax.ppermute(v, axis, [(i, partner(i, parity)) for i in range(RING)])


def pair_x(v, flip, cross):
    route = [(x * 2 + p, (x ^ flip) * 2 + (p ^ cross)) for x in range(X) for p in range(2)]
    return lax.ppermute(v, ("x", "pp"), route)


def swap(v):
    return lax.ppermute(v, "pp", [(0, 1), (1, 0)])


def shift_ctx(v, by, cross):
    n = RING * X
    route = []
    for i in range(n):
        for p in range(2):
            if 0 <= i + by < n:
                route.append((i * 2 + p, (i + by) * 2 + (p ^ cross)))
    return lax.ppermute(v, ("z", "x", "pp"), route)


def join_kernel(own, first, out):
    out[0] = own[...]
    out[1] = first[...]


def join(own, first):
    return pl.pallas_call(
        join_kernel,
        out_shape=jax.ShapeDtypeStruct((2,) + own.shape, BF),
        in_specs=vmem(2),
        out_specs=vmem(1)[0],
        compiler_params=params(2),
        cost_estimate=pl.CostEstimate(flops=1 << 10, bytes_accessed=1 << 18, transcendentals=0),
        name="join",
    )(own, first)


def gather_ring(halves, axis):
    def hop(n, turn, v):
        return pair_ring(v, axis, (n + turn) % 2)

    firsts = [hop(n, 0, halves[n]) for n in range(2)]
    held = [[join(halves[n], firsts[n]) for n in range(2)]]
    for turn in (1, 2, 3):
        now = lax.optimization_barrier(held[-1])
        held.append([hop(n, turn, now[n]) for n in range(2)])
    return held


def place_rows(mine, even, odd, full_ref):
    x, side = lax.axis_index("x"), lax.axis_index("yb")
    rows = mine.shape[2]
    for m in range(X):
        top = pl.multiple_of(jnp.bitwise_xor(m, x) * rows, rows)
        there = even[m] if m < X // 2 else odd[m - X // 2]
        for k in range(RING // 2):
            at = pl.multiple_of((2 * k + side) * LANES, LANES)
            full_ref[pl.ds(top, rows), pl.ds(at, LANES)] = mine[m, k]
            at = pl.multiple_of((2 * k + 1 - side) * LANES, LANES)
            full_ref[pl.ds(top, rows), pl.ds(at, LANES)] = there[k]


def place(held, full_ref, me):
    rows = full_ref.shape[0] // 2
    for n in range(2):
        step = jnp.where(lax.rem(me, 2) == n, 1, -1)
        spots = [(0, step), (-step, -2 * step), (2 * step, 3 * step), (-3 * step, -4 * step)]
        for turn in range(4):
            for k in range(2):
                index = lax.rem(me + spots[turn][k] + 2 * RING, RING)
                at = pl.multiple_of(index * LANES, LANES)
                full_ref[n * rows : (n + 1) * rows, pl.ds(at, LANES)] = held[turn * 2 + n][k]


def matmul_kernel(*refs):
    a_held, b_held, outs, (a_full, b_full) = refs[:3], refs[3:11], refs[11:15], refs[15:]
    send_head, send_tail, keep_head, keep_tail = outs
    place_rows(*a_held, a_full)
    place(b_held, b_full, lax.axis_index("z"))
    rows = a_full.shape[0] // X
    width = 2 * LANES

    def columns(c, carry):
        at = pl.multiple_of(c * width, width)
        product = lax.dot_general(
            a_full[...],
            b_full[pl.ds(at, width), :],
            (((1,), (1,)), ((), ())),
            preferred_element_type=F32,
        )
        own, near, across, far = [product[n * rows : (n + 1) * rows] for n in range(X)]
        here = pl.ds(at, width)
        send_head[0, :, here] = near[:HEAD].astype(BF)
        send_head[1, :, here] = across[:HEAD].astype(BF)
        send_tail[0, :, here] = far[HEAD:].astype(BF)
        send_tail[1, :, here] = across[HEAD:].astype(BF)
        keep_head[0, :, here] = own[:HEAD]
        keep_head[1, :, here] = far[:HEAD]
        keep_tail[0, :, here] = own[HEAD:]
        keep_tail[1, :, here] = near[HEAD:]
        return carry

    lax.fori_loop(0, b_full.shape[0] // width, columns, 0)


def partial_products(a_held, b_held):
    b_list = [v for parts in b_held for v in parts]
    rows = X * a_held[0].shape[2]
    cols = 2 * b_list[0].shape[1]
    depth = RING * LANES
    head = (2, HEAD, cols)
    tail = (2, rows // X - HEAD, cols)
    return pl.pallas_call(
        matmul_kernel,
        out_shape=[
            jax.ShapeDtypeStruct(head, BF),
            jax.ShapeDtypeStruct(tail, BF),
            jax.ShapeDtypeStruct(head, F32),
            jax.ShapeDtypeStruct(tail, F32),
        ],
        in_specs=vmem(11),
        out_specs=vmem(4),
        scratch_shapes=[pltpu.VMEM((rows, depth), BF), pltpu.VMEM((cols, depth), BF)],
        compiler_params=params(10),
        cost_estimate=pl.CostEstimate(
            flops=2 * rows * cols * depth, bytes_accessed=8 << 20, transcendentals=0
        ),
        name="partial_products",
    )(*a_held, *b_list)


def fold_kernel(keep_head, got_head, keep_tail, got_tail, out_head, out_tail, own):
    out_head[...] = (keep_head[1] + got_head[1].astype(F32)).astype(BF)
    out_tail[...] = (keep_tail[1] + got_tail[1].astype(F32)).astype(BF)
    own[0:HEAD] = (keep_head[0] + got_head[0].astype(F32)).astype(BF)
    own[HEAD:] = (keep_tail[0] + got_tail[0].astype(F32)).astype(BF)


def fold(keep_head, got_head, keep_tail, got_tail):
    head, tail = got_head.shape[1:], got_tail.shape[1:]
    return pl.pallas_call(
        fold_kernel,
        out_shape=[
            jax.ShapeDtypeStruct(head, BF),
            jax.ShapeDtypeStruct(tail, BF),
            jax.ShapeDtypeStruct((head[0] + tail[0], head[1]), BF),
        ],
        in_specs=vmem(4),
        out_specs=vmem(3),
        compiler_params=params(2),
        cost_estimate=pl.CostEstimate(flops=1 << 18, bytes_accessed=4 << 20, transcendentals=0),
        name="fold",
    )(keep_head, got_head, keep_tail, got_tail)


def quarter_kernel(cotangent, out):
    for x in range(X):
        quarter = cotangent[:, x * LANES : (x + 1) * LANES]
        for k in range(RING // 2):
            out[x, k] = quarter


def quarters_of(cotangent):
    return pl.pallas_call(
        quarter_kernel,
        out_shape=jax.ShapeDtypeStruct((X, RING // 2, cotangent.shape[0], LANES), BF),
        in_specs=vmem(1),
        out_specs=vmem(1)[0],
        compiler_params=params(2),
        cost_estimate=pl.CostEstimate(flops=1 << 10, bytes_accessed=1 << 20, transcendentals=0),
        name="quarters",
    )(cotangent)


def lane_tile(index):
    return pl.ds(pl.multiple_of(index * LANES, LANES), LANES)


def tail_kernel(feats, taps, out, ext):
    rows = feats.shape[1]
    keep = rows - LANES

    def tile(l, carry):
        at = lane_tile(l)
        mixed = []
        for i in (1, 2):
            ext[...] = feats[i, keep - 16 : rows, at].astype(F32)
            mixed.append(
                taps[i : i + 1, at] * ext[16 : 16 + LANES]
                + taps[3 + i : 4 + i, at] * ext[15 : 15 + LANES]
                + taps[6 + i : 7 + i, at] * ext[14 : 14 + LANES]
            )
        out[0:LANES, at] = (mixed[0] * mixed[1]).astype(BF)
        last = [feats[i, rows - 16 : rows, at].astype(F32)[14:16] for i in range(3)]
        last.append(jnp.zeros((10, LANES), F32))
        out[LANES:HALO, at] = jnp.concatenate(last, axis=0).astype(BF)
        return carry

    lax.fori_loop(0, feats.shape[2] // LANES, tile, 0)


def tail_rows(feats, taps):
    channels = feats.shape[2]
    return pl.pallas_call(
        tail_kernel,
        out_shape=jax.ShapeDtypeStruct((HALO, channels), BF),
        in_specs=vmem(2),
        out_specs=vmem(1)[0],
        scratch_shapes=[pltpu.VMEM((LANES + 16, LANES), F32)],
        compiler_params=params(8),
        cost_estimate=pl.CostEstimate(flops=1 << 20, bytes_accessed=2 << 20, transcendentals=0),
        name="tail_rows",
    )(feats, taps)


def pick_groups(product, per_tile, width):
    rows = product.shape[0] // per_tile
    shape = (rows, product.shape[1])
    group = lax.rem(lax.broadcasted_iota(jnp.int32, shape, 1), LANES) // width
    out = product[:rows]
    for g in range(1, per_tile):
        out = jnp.where(group == g, product[g * rows : (g + 1) * rows], out)
    return out


def forward_kernel(feats, taps, filters, halo, conv, gate, key, value, back, fwd_band, flipped, plain, ext):
    rows = feats.shape[1]
    groups = filters.shape[0]
    per_tile = groups * LANES // feats.shape[2]
    width = LANES // per_tile
    row = lax.broadcasted_iota(jnp.int32, (LANES, LANES), 0)
    col = lax.broadcasted_iota(jnp.int32, (LANES, LANES), 1)
    mirror = jnp.where(lax.rem(row + col, LANES) == 0, 1.0, 0.0).astype(BF)
    flipped[...] = jnp.dot(filters[...], mirror, preferred_element_type=F32)
    plain[...] = filters[...].astype(F32)

    def tile(l, carry):
        at = lane_tile(l)
        for g in range(per_tile):
            index = l * per_tile + g
            spread = jnp.broadcast_to(plain[pl.ds(index, 1), :], (LANES, LANES))
            turned = pltpu.roll(spread, 0, 1, stride=1, stride_axis=0)
            back[index, :, 0:LANES] = jnp.where(col >= row, turned, 0.0).astype(BF)
            back[index, :, LANES : 2 * LANES] = jnp.where(col < row, turned, 0.0).astype(BF)
            spread = jnp.broadcast_to(flipped[pl.ds(index, 1), :], (LANES, LANES))
            turned = pltpu.roll(spread, 0, 1, stride=1, stride_axis=0)
            fwd_band[g * LANES : (g + 1) * LANES, 0:LANES] = jnp.where(col > row, turned, 0.0).astype(BF)
            fwd_band[g * LANES : (g + 1) * LANES, LANES : 2 * LANES] = jnp.where(
                col <= row, turned, 0.0
            ).astype(BF)
        before = halo[LANES:HALO, at].astype(F32)
        mixed = []
        for i in range(3):
            ext[0:8] = jnp.concatenate([jnp.zeros((6, LANES), F32), before[2 * i : 2 * i + 2]], axis=0)
            ext[8 : 8 + rows] = feats[i, :, at].astype(F32)
            mixed.append(
                taps[i : i + 1, at] * ext[8 : 8 + rows]
                + taps[3 + i : 4 + i, at] * ext[7 : 7 + rows]
                + taps[6 + i : 7 + i, at] * ext[6 : 6 + rows]
            )
        gate[:, at] = mixed[0]
        key[:, at] = mixed[1]
        value[:, at] = mixed[2]
        products = (mixed[1] * mixed[2]).astype(BF)
        first = jnp.concatenate([halo[0:LANES, at], products[:LANES]], axis=0)
        window = jnp.concatenate([first, products], axis=1)
        picked = pick_groups(
            jnp.dot(fwd_band[...], window, preferred_element_type=F32), per_tile, width
        )
        conv[0:LANES, at] = picked[:, :LANES]
        conv[LANES : 2 * LANES, at] = picked[:, LANES:]
        return carry

    lax.fori_loop(0, feats.shape[2] // LANES, tile, 0)


def forward_part(feats, taps, filters, halo):
    _, rows, channels = feats.shape
    groups = filters.shape[0]
    full = jax.ShapeDtypeStruct((rows, channels), F32)
    per_tile = groups * LANES // channels
    return pl.pallas_call(
        forward_kernel,
        out_shape=[full] * 4 + [jax.ShapeDtypeStruct((groups, LANES, 2 * LANES), BF)],
        in_specs=vmem(4),
        out_specs=vmem(5),
        scratch_shapes=[
            pltpu.VMEM((per_tile * LANES, 2 * LANES), BF),
            pltpu.VMEM((groups, LANES), F32),
            pltpu.VMEM((groups, LANES), F32),
            pltpu.VMEM((rows + 8, LANES), F32),
        ],
        compiler_params=params(8),
        cost_estimate=pl.CostEstimate(flops=2 << 30, bytes_accessed=12 << 20, transcendentals=0),
        name="forward_part",
    )(feats, taps, filters, halo)


def gated(own, last, conv, gate, grad_conv, grad_gate):
    grad_y = (own.astype(F32) + last[...].astype(F32)).astype(BF).astype(F32)
    down = (grad_y * gate).astype(BF)
    across = (grad_y * conv).astype(BF)
    grad_conv[...] = down
    grad_gate[...] = across
    return down, across


def head_kernel(own, last, conv, gate, feats, grad_conv, grad_gate, halo):
    down, across = gated(own[0:HEAD], last, conv[0:HEAD], gate[0:HEAD], grad_conv, grad_gate)
    halo[0:LANES] = down[0:LANES]
    pieces = [
        down[LANES:HEAD].astype(F32)[0:1],
        across[0:16].astype(F32)[0:2],
        feats[1, 0:16].astype(F32)[0:2],
        feats[2, 0:16].astype(F32)[0:2],
        jnp.zeros((9, down.shape[1]), F32),
    ]
    halo[LANES:HALO] = jnp.concatenate(pieces, axis=0).astype(BF)


def tail_gate_kernel(own, last, conv, gate, grad_conv, grad_gate):
    rows = conv.shape[0]
    gated(own[HEAD:rows], last, conv[HEAD:rows], gate[HEAD:rows], grad_conv, grad_gate)


def gate_head(own, last, conv, gate, feats):
    half = jax.ShapeDtypeStruct(last.shape, BF)
    return pl.pallas_call(
        head_kernel,
        out_shape=[half, half, jax.ShapeDtypeStruct((HALO, last.shape[1]), BF)],
        in_specs=vmem(5),
        out_specs=vmem(3),
        compiler_params=params(8),
        cost_estimate=pl.CostEstimate(flops=1 << 20, bytes_accessed=3 << 20, transcendentals=0),
        name="gate_head",
    )(own, last, conv, gate, feats)


def gate_tail(own, last, conv, gate):
    half = jax.ShapeDtypeStruct(last.shape, BF)
    return pl.pallas_call(
        tail_gate_kernel,
        out_shape=[half, half],
        in_specs=vmem(4),
        out_specs=vmem(2),
        compiler_params=params(8),
        cost_estimate=pl.CostEstimate(flops=1 << 20, bytes_accessed=3 << 20, transcendentals=0),
        name="gate_tail",
    )(own, last, conv, gate)


def final_kernel(
    conv_head, conv_tail, gate_head, gate_tail, halo, key, value, feats, taps, back, out, ext, small
):
    rows = key.shape[0]
    groups = back.shape[0]
    per_tile = groups * LANES // key.shape[1]
    width = LANES // per_tile

    def tile(l, carry):
        at = lane_tile(l)
        mine = jnp.concatenate([conv_head[:, at], conv_tail[:, at]], axis=0)
        after = halo[0:LANES, at]
        second = jnp.concatenate([mine[LANES:], after], axis=0)
        window = jnp.concatenate([mine, second], axis=1)
        first_group = pl.multiple_of(l * per_tile, per_tile)
        band = back[pl.ds(first_group, per_tile)]
        picked = pick_groups(
            jnp.dot(
                band.reshape(per_tile * LANES, 2 * LANES), window, preferred_element_type=F32
            ),
            per_tile,
            width,
        )
        rim = halo[LANES:HALO, at]
        beyond = jnp.concatenate([after, rim, jnp.zeros((LANES - 16, LANES), BF)], axis=0)
        top = band[:, 0:16, :].reshape(per_tile * 16, 2 * LANES)
        extra = pick_groups(jnp.dot(top, beyond, preferred_element_type=F32), per_tile, width)[0:2]
        rim_f = rim.astype(F32)
        streams = []
        for i, stream in ((1, value), (2, key)):
            other = 3 - i
            small[0:8] = feats[other, rows - 16 : rows, at].astype(F32)[8:16]
            small[8:16] = jnp.concatenate(
                [rim_f[1 + 2 * other : 3 + 2 * other], jnp.zeros((6, LANES), F32)], axis=0
            )
            beyond_mixed = (
                taps[other : other + 1, at] * small[8:10]
                + taps[3 + other : 4 + other, at] * small[7:9]
                + taps[6 + other : 7 + other, at] * small[6:8]
            )
            streams.append((i, stream, (extra * beyond_mixed).astype(BF).astype(F32)))

        def finish(i, mix_beyond):
            ext[rows : rows + 8] = jnp.concatenate([mix_beyond, jnp.zeros((6, LANES), F32)], axis=0)
            result = (
                taps[i : i + 1, at] * ext[0:rows]
                + taps[3 + i : 4 + i, at] * ext[1 : rows + 1]
                + taps[6 + i : 7 + i, at] * ext[2 : rows + 2]
            )
            out[i, :, at] = result.astype(BF)

        ext[0:HEAD] = gate_head[:, at].astype(F32)
        ext[HEAD:rows] = gate_tail[:, at].astype(F32)
        finish(0, rim_f[1:3])
        for i, stream, mix_beyond in streams:
            ext[0:LANES] = (picked[:, :LANES] * stream[0:LANES, at]).astype(BF).astype(F32)
            ext[LANES : 2 * LANES] = (
                (picked[:, LANES:] * stream[LANES : 2 * LANES, at]).astype(BF).astype(F32)
            )
            finish(i, mix_beyond)
        return carry

    lax.fori_loop(0, key.shape[1] // LANES, tile, 0)


def final_part(convs, gates, halo, key, value, feats, taps, back):
    rows, channels = key.shape
    return pl.pallas_call(
        final_kernel,
        out_shape=jax.ShapeDtypeStruct((3, rows, channels), BF),
        in_specs=vmem(10),
        out_specs=vmem(1)[0],
        scratch_shapes=[pltpu.VMEM((rows + 8, LANES), F32), pltpu.VMEM((16, LANES), F32)],
        compiler_params=params(8),
        cost_estimate=pl.CostEstimate(flops=2 << 30, bytes_accessed=12 << 20, transcendentals=0),
        name="final_part",
    )(*convs, *gates, halo, key, value, feats, taps, back)


def after(value, *others):
    return lax.optimization_barrier((value,) + others)[0]


def spread(quarters):
    flat = quarters.reshape((X * RING // 2,) + quarters.shape[2:])
    return lax.all_to_all(flat, ("x", "yq"), 0, 0).reshape(quarters.shape)


def local(features, short_taps, long_filters, out_weight, out_grad):
    feats = jnp.transpose(features[0], (1, 0, 2))
    _, channels = feats.shape[1:]
    taps = short_taps[0].reshape(9, channels)
    filters = jnp.transpose(long_filters[0])

    quarters = quarters_of(out_grad[0])
    weight = after(out_weight[0], quarters)
    b_held = gather_ring([weight[: channels // 2], weight[channels // 2 :]], "z")
    mine = spread(quarters)
    even = pair_ring(mine[: X // 2], ("yq", "yb"), 0)
    odd = pair_ring(mine[X // 2 :], ("yq", "yb"), 1)
    a_held = (mine, even, odd)
    halo_before = shift_ctx(tail_rows(feats, taps), 1, 1)
    feats = swap(feats)
    taps = swap(taps)
    filters = swap(filters)
    conv, gate, key, value, back = forward_part(feats, taps, filters, halo_before)

    send_head, send_tail, keep_head, keep_tail = partial_products(a_held, b_held)
    got_head = pair_x(send_head, 1, 0)
    got_tail = pair_x(send_tail, 3, 0)
    head, tail, own = fold(keep_head, got_head, keep_tail, got_tail)
    last_head = pair_x(head, 3, 1)
    last_tail = pair_x(tail, 1, 1)
    own = swap(own)
    conv_head, cross_head, halo = gate_head(own, last_head, conv, gate, feats)
    conv_tail, cross_tail = gate_tail(own, last_tail, conv, gate)
    halo_after = shift_ctx(halo, -1, 0)
    grad_feat = final_part(
        (conv_head, conv_tail), (cross_head, cross_tail), halo_after, key, value, feats, taps, back
    )
    return jnp.transpose(grad_feat, (1, 0, 2))[None]


def solution(mesh):
    parts = jax.sharding.Mesh(
        mesh.devices.reshape(RING, X, RING // 2, 2, 2),
        ("z", "x", "yq", "yb", "pp"),
        axis_types=(jax.sharding.AxisType.Auto,) * 5,
    )
    ctx, tp = ("z", "x"), ("yq", "yb")
    in_specs = (
        P("pp", ctx, None, tp),
        P("pp", None, None, tp),
        P("pp", None, tp),
        P("pp", tp, ctx),
        P("pp", ctx, tp),
    )
    out_specs = P("pp", ctx, None, tp)

    return jax.shard_map(local, mesh=parts, in_specs=in_specs, out_specs=out_specs, check_vma=False)
```

```python
import jax
import jax.numpy as jnp
from jax import lax
from jax.experimental import pallas as pl
from jax.experimental.pallas import tpu as pltpu
from jax.sharding import PartitionSpec as P

BF = jnp.bfloat16
F32 = jnp.float32
LANES = 128
X = 4
RING = 8
HALO = 144
HEAD = 144


def vmem(n):
    return [pl.BlockSpec(memory_space=pltpu.VMEM)] * n


def params(mib):
    return pltpu.CompilerParams(vmem_limit_bytes=mib << 20)


def partner(i, parity):
    return (i + 1) % RING if i % 2 == parity else (i - 1) % RING


def pair_ring(v, axis, parity):
    return lax.ppermute(v, axis, [(i, partner(i, parity)) for i in range(RING)])


def pair_x(v, flip, cross):
    route = [(x * 2 + p, (x ^ flip) * 2 + (p ^ cross)) for x in range(X) for p in range(2)]
    return lax.ppermute(v, ("x", "pp"), route)


def swap(v):
    return lax.ppermute(v, "pp", [(0, 1), (1, 0)])


def shift_ctx(v, by, cross):
    n = RING * X
    route = []
    for i in range(n):
        for p in range(2):
            if 0 <= i + by < n:
                route.append((i * 2 + p, (i + by) * 2 + (p ^ cross)))
    return lax.ppermute(v, ("z", "x", "pp"), route)


def join_kernel(own, first, out):
    out[0] = own[...]
    out[1] = first[...]


def join(own, first):
    return pl.pallas_call(
        join_kernel,
        out_shape=jax.ShapeDtypeStruct((2,) + own.shape, BF),
        in_specs=vmem(2),
        out_specs=vmem(1)[0],
        compiler_params=params(2),
        cost_estimate=pl.CostEstimate(flops=1 << 10, bytes_accessed=1 << 18, transcendentals=0),
        name="join",
    )(own, first)


def gather_ring(halves, axis):
    def hop(n, turn, v):
        return pair_ring(v, axis, (n + turn) % 2)

    firsts = [hop(n, 0, halves[n]) for n in range(2)]
    held = [[join(halves[n], firsts[n]) for n in range(2)]]
    for turn in (1, 2, 3):
        now = lax.optimization_barrier(held[-1])
        held.append([hop(n, turn, now[n]) for n in range(2)])
    return held


def place_rows(mine, even, odd, head, tail):
    x, side = lax.axis_index("x"), lax.axis_index("yb")
    rest = mine.shape[2] - HEAD

    def put(value, slot, y):
        at = pl.ds(pl.multiple_of(y * LANES, LANES), LANES)
        head[pl.ds(pl.multiple_of(slot * HEAD, 16), HEAD), at] = value[:HEAD]
        tail[pl.ds(pl.multiple_of(slot * rest, 16), rest), at] = value[HEAD:]

    for m in range(X):
        slot = jnp.bitwise_xor(m, x)
        there = even[m] if m < X // 2 else odd[m - X // 2]
        for k in range(RING // 2):
            put(mine[m, k], slot, 2 * k + side)
            put(there[k], slot, 2 * k + 1 - side)


def place(held, full_ref, me):
    rows = full_ref.shape[0] // 2
    for n in range(2):
        step = jnp.where(lax.rem(me, 2) == n, 1, -1)
        spots = [(0, step), (-step, -2 * step), (2 * step, 3 * step), (-3 * step, -4 * step)]
        for turn in range(4):
            for k in range(2):
                index = lax.rem(me + spots[turn][k] + 2 * RING, RING)
                at = pl.multiple_of(index * LANES, LANES)
                full_ref[n * rows : (n + 1) * rows, pl.ds(at, LANES)] = held[turn * 2 + n][k]


def multiply(rows_ref, b_full, store):
    size = rows_ref.shape[0] // X
    width = 2 * LANES

    def columns(c, carry):
        at = pl.ds(pl.multiple_of(c * width, width), width)
        product = lax.dot_general(
            rows_ref[...], b_full[at, :], (((1,), (1,)), ((), ())), preferred_element_type=F32
        )
        store(at, *[product[n * size : (n + 1) * size] for n in range(X)])
        return carry

    lax.fori_loop(0, b_full.shape[0] // width, columns, 0)


def head_product_kernel(*refs):
    a_held, b_held, (send, keep, a_tail, b_full), (a_head,) = refs[:3], refs[3:11], refs[11:15], refs[15:]
    place_rows(*a_held, a_head, a_tail)
    place(b_held, b_full, lax.axis_index("z"))

    def store(at, own, near, across, far):
        send[0, :, at] = near.astype(BF)
        send[1, :, at] = across.astype(BF)
        keep[0, :, at] = own
        keep[1, :, at] = far

    multiply(a_head, b_full, store)


def tail_product_kernel(a_tail, b_full, send, keep):
    def store(at, own, near, across, far):
        send[0, :, at] = far.astype(BF)
        send[1, :, at] = across.astype(BF)
        keep[0, :, at] = own
        keep[1, :, at] = near

    multiply(a_tail, b_full, store)


def head_products(a_held, b_held):
    b_list = [v for parts in b_held for v in parts]
    rest = a_held[0].shape[2] - HEAD
    cols = 2 * b_list[0].shape[1]
    depth = RING * LANES
    return pl.pallas_call(
        head_product_kernel,
        out_shape=[
            jax.ShapeDtypeStruct((2, HEAD, cols), BF),
            jax.ShapeDtypeStruct((2, HEAD, cols), F32),
            jax.ShapeDtypeStruct((X * rest, depth), BF),
            jax.ShapeDtypeStruct((cols, depth), BF),
        ],
        in_specs=vmem(11),
        out_specs=vmem(4),
        scratch_shapes=[pltpu.VMEM((X * HEAD, depth), BF)],
        compiler_params=params(8),
        cost_estimate=pl.CostEstimate(flops=1 << 30, bytes_accessed=8 << 20, transcendentals=0),
        name="head_products",
    )(*a_held, *b_list)


def tail_products(a_tail, b_full):
    shape = (2, a_tail.shape[0] // X, b_full.shape[0])
    return pl.pallas_call(
        tail_product_kernel,
        out_shape=[jax.ShapeDtypeStruct(shape, BF), jax.ShapeDtypeStruct(shape, F32)],
        in_specs=vmem(2),
        out_specs=vmem(2),
        compiler_params=params(8),
        cost_estimate=pl.CostEstimate(flops=1 << 30, bytes_accessed=4 << 20, transcendentals=0),
        name="tail_products",
    )(a_tail, b_full)


def fold_kernel(keep_head, got_head, keep_tail, got_tail, out_head, out_tail, own):
    out_head[...] = (keep_head[1] + got_head[1].astype(F32)).astype(BF)
    out_tail[...] = (keep_tail[1] + got_tail[1].astype(F32)).astype(BF)
    own[0:HEAD] = (keep_head[0] + got_head[0].astype(F32)).astype(BF)
    own[HEAD:] = (keep_tail[0] + got_tail[0].astype(F32)).astype(BF)


def fold(keep_head, got_head, keep_tail, got_tail):
    head, tail = got_head.shape[1:], got_tail.shape[1:]
    return pl.pallas_call(
        fold_kernel,
        out_shape=[
            jax.ShapeDtypeStruct(head, BF),
            jax.ShapeDtypeStruct(tail, BF),
            jax.ShapeDtypeStruct((head[0] + tail[0], head[1]), BF),
        ],
        in_specs=vmem(4),
        out_specs=vmem(3),
        compiler_params=params(2),
        cost_estimate=pl.CostEstimate(flops=1 << 18, bytes_accessed=4 << 20, transcendentals=0),
        name="fold",
    )(keep_head, got_head, keep_tail, got_tail)


def quarter_kernel(cotangent, out):
    for x in range(X):
        quarter = cotangent[:, x * LANES : (x + 1) * LANES]
        for k in range(RING // 2):
            out[x, k] = quarter


def quarters_of(cotangent):
    return pl.pallas_call(
        quarter_kernel,
        out_shape=jax.ShapeDtypeStruct((X, RING // 2, cotangent.shape[0], LANES), BF),
        in_specs=vmem(1),
        out_specs=vmem(1)[0],
        compiler_params=params(2),
        cost_estimate=pl.CostEstimate(flops=1 << 10, bytes_accessed=1 << 20, transcendentals=0),
        name="quarters",
    )(cotangent)


def lane_tile(index):
    return pl.ds(pl.multiple_of(index * LANES, LANES), LANES)


def tail_kernel(feats, taps, out, ext):
    rows = feats.shape[1]
    keep = rows - LANES

    def tile(l, carry):
        at = lane_tile(l)
        mixed = []
        for i in (1, 2):
            ext[...] = feats[i, keep - 16 : rows, at].astype(F32)
            mixed.append(
                taps[i : i + 1, at] * ext[16 : 16 + LANES]
                + taps[3 + i : 4 + i, at] * ext[15 : 15 + LANES]
                + taps[6 + i : 7 + i, at] * ext[14 : 14 + LANES]
            )
        out[0:LANES, at] = (mixed[0] * mixed[1]).astype(BF)
        last = [feats[i, rows - 16 : rows, at].astype(F32)[14:16] for i in range(3)]
        last.append(jnp.zeros((10, LANES), F32))
        out[LANES:HALO, at] = jnp.concatenate(last, axis=0).astype(BF)
        return carry

    lax.fori_loop(0, feats.shape[2] // LANES, tile, 0)


def tail_rows(feats, taps):
    channels = feats.shape[2]
    return pl.pallas_call(
        tail_kernel,
        out_shape=jax.ShapeDtypeStruct((HALO, channels), BF),
        in_specs=vmem(2),
        out_specs=vmem(1)[0],
        scratch_shapes=[pltpu.VMEM((LANES + 16, LANES), F32)],
        compiler_params=params(8),
        cost_estimate=pl.CostEstimate(flops=1 << 20, bytes_accessed=2 << 20, transcendentals=0),
        name="tail_rows",
    )(feats, taps)


def pick_groups(product, per_tile, width):
    rows = product.shape[0] // per_tile
    shape = (rows, product.shape[1])
    group = lax.rem(lax.broadcasted_iota(jnp.int32, shape, 1), LANES) // width
    out = product[:rows]
    for g in range(1, per_tile):
        out = jnp.where(group == g, product[g * rows : (g + 1) * rows], out)
    return out


def forward_kernel(feats, taps, filters, halo, conv, gate, key, value, back, fwd_band, flipped, plain, ext):
    rows = feats.shape[1]
    groups = filters.shape[0]
    per_tile = groups * LANES // feats.shape[2]
    width = LANES // per_tile
    row = lax.broadcasted_iota(jnp.int32, (LANES, LANES), 0)
    col = lax.broadcasted_iota(jnp.int32, (LANES, LANES), 1)
    mirror = jnp.where(lax.rem(row + col, LANES) == 0, 1.0, 0.0).astype(BF)
    flipped[...] = jnp.dot(filters[...], mirror, preferred_element_type=F32)
    plain[...] = filters[...].astype(F32)

    def tile(l, carry):
        at = lane_tile(l)
        for g in range(per_tile):
            index = l * per_tile + g
            spread = jnp.broadcast_to(plain[pl.ds(index, 1), :], (LANES, LANES))
            turned = pltpu.roll(spread, 0, 1, stride=1, stride_axis=0)
            back[index, :, 0:LANES] = jnp.where(col >= row, turned, 0.0).astype(BF)
            back[index, :, LANES : 2 * LANES] = jnp.where(col < row, turned, 0.0).astype(BF)
            spread = jnp.broadcast_to(flipped[pl.ds(index, 1), :], (LANES, LANES))
            turned = pltpu.roll(spread, 0, 1, stride=1, stride_axis=0)
            fwd_band[g * LANES : (g + 1) * LANES, 0:LANES] = jnp.where(col > row, turned, 0.0).astype(BF)
            fwd_band[g * LANES : (g + 1) * LANES, LANES : 2 * LANES] = jnp.where(
                col <= row, turned, 0.0
            ).astype(BF)
        before = halo[LANES:HALO, at].astype(F32)
        mixed = []
        for i in range(3):
            ext[0:8] = jnp.concatenate([jnp.zeros((6, LANES), F32), before[2 * i : 2 * i + 2]], axis=0)
            ext[8 : 8 + rows] = feats[i, :, at].astype(F32)
            mixed.append(
                taps[i : i + 1, at] * ext[8 : 8 + rows]
                + taps[3 + i : 4 + i, at] * ext[7 : 7 + rows]
                + taps[6 + i : 7 + i, at] * ext[6 : 6 + rows]
            )
        gate[:, at] = mixed[0]
        key[:, at] = mixed[1]
        value[:, at] = mixed[2]
        products = (mixed[1] * mixed[2]).astype(BF)
        first = jnp.concatenate([halo[0:LANES, at], products[:LANES]], axis=0)
        window = jnp.concatenate([first, products], axis=1)
        picked = pick_groups(
            jnp.dot(fwd_band[...], window, preferred_element_type=F32), per_tile, width
        )
        conv[0:LANES, at] = picked[:, :LANES]
        conv[LANES : 2 * LANES, at] = picked[:, LANES:]
        return carry

    lax.fori_loop(0, feats.shape[2] // LANES, tile, 0)


def forward_part(feats, taps, filters, halo):
    _, rows, channels = feats.shape
    groups = filters.shape[0]
    full = jax.ShapeDtypeStruct((rows, channels), F32)
    per_tile = groups * LANES // channels
    return pl.pallas_call(
        forward_kernel,
        out_shape=[full] * 4 + [jax.ShapeDtypeStruct((groups, LANES, 2 * LANES), BF)],
        in_specs=vmem(4),
        out_specs=vmem(5),
        scratch_shapes=[
            pltpu.VMEM((per_tile * LANES, 2 * LANES), BF),
            pltpu.VMEM((groups, LANES), F32),
            pltpu.VMEM((groups, LANES), F32),
            pltpu.VMEM((rows + 8, LANES), F32),
        ],
        compiler_params=params(8),
        cost_estimate=pl.CostEstimate(flops=2 << 30, bytes_accessed=12 << 20, transcendentals=0),
        name="forward_part",
    )(feats, taps, filters, halo)


def gated(own, last, conv, gate, grad_conv, grad_gate):
    grad_y = (own.astype(F32) + last[...].astype(F32)).astype(BF).astype(F32)
    down = (grad_y * gate).astype(BF)
    across = (grad_y * conv).astype(BF)
    grad_conv[...] = down
    grad_gate[...] = across
    return down, across


def head_kernel(own, last, conv, gate, feats, grad_conv, grad_gate, halo):
    down, across = gated(own[0:HEAD], last, conv[0:HEAD], gate[0:HEAD], grad_conv, grad_gate)
    halo[0:LANES] = down[0:LANES]
    pieces = [
        down[LANES:HEAD].astype(F32)[0:1],
        across[0:16].astype(F32)[0:2],
        feats[1, 0:16].astype(F32)[0:2],
        feats[2, 0:16].astype(F32)[0:2],
        jnp.zeros((9, down.shape[1]), F32),
    ]
    halo[LANES:HALO] = jnp.concatenate(pieces, axis=0).astype(BF)


def tail_gate_kernel(own, last, conv, gate, grad_conv, grad_gate):
    rows = conv.shape[0]
    gated(own[HEAD:rows], last, conv[HEAD:rows], gate[HEAD:rows], grad_conv, grad_gate)


def gate_head(own, last, conv, gate, feats):
    half = jax.ShapeDtypeStruct(last.shape, BF)
    return pl.pallas_call(
        head_kernel,
        out_shape=[half, half, jax.ShapeDtypeStruct((HALO, last.shape[1]), BF)],
        in_specs=vmem(5),
        out_specs=vmem(3),
        compiler_params=params(8),
        cost_estimate=pl.CostEstimate(flops=1 << 20, bytes_accessed=3 << 20, transcendentals=0),
        name="gate_head",
    )(own, last, conv, gate, feats)


def gate_tail(own, last, conv, gate):
    half = jax.ShapeDtypeStruct(last.shape, BF)
    return pl.pallas_call(
        tail_gate_kernel,
        out_shape=[half, half],
        in_specs=vmem(4),
        out_specs=vmem(2),
        compiler_params=params(8),
        cost_estimate=pl.CostEstimate(flops=1 << 20, bytes_accessed=3 << 20, transcendentals=0),
        name="gate_tail",
    )(own, last, conv, gate)


def final_kernel(
    conv_head, conv_tail, gate_head, gate_tail, halo, key, value, feats, taps, back, out, ext, small
):
    rows = key.shape[0]
    groups = back.shape[0]
    per_tile = groups * LANES // key.shape[1]
    width = LANES // per_tile

    def tile(l, carry):
        at = lane_tile(l)
        mine = jnp.concatenate([conv_head[:, at], conv_tail[:, at]], axis=0)
        after = halo[0:LANES, at]
        second = jnp.concatenate([mine[LANES:], after], axis=0)
        window = jnp.concatenate([mine, second], axis=1)
        first_group = pl.multiple_of(l * per_tile, per_tile)
        band = back[pl.ds(first_group, per_tile)]
        picked = pick_groups(
            jnp.dot(
                band.reshape(per_tile * LANES, 2 * LANES), window, preferred_element_type=F32
            ),
            per_tile,
            width,
        )
        rim = halo[LANES:HALO, at]
        beyond = jnp.concatenate([after, rim, jnp.zeros((LANES - 16, LANES), BF)], axis=0)
        top = band[:, 0:16, :].reshape(per_tile * 16, 2 * LANES)
        extra = pick_groups(jnp.dot(top, beyond, preferred_element_type=F32), per_tile, width)[0:2]
        rim_f = rim.astype(F32)
        streams = []
        for i, stream in ((1, value), (2, key)):
            other = 3 - i
            small[0:8] = feats[other, rows - 16 : rows, at].astype(F32)[8:16]
            small[8:16] = jnp.concatenate(
                [rim_f[1 + 2 * other : 3 + 2 * other], jnp.zeros((6, LANES), F32)], axis=0
            )
            beyond_mixed = (
                taps[other : other + 1, at] * small[8:10]
                + taps[3 + other : 4 + other, at] * small[7:9]
                + taps[6 + other : 7 + other, at] * small[6:8]
            )
            streams.append((i, stream, (extra * beyond_mixed).astype(BF).astype(F32)))

        def finish(i, mix_beyond):
            ext[rows : rows + 8] = jnp.concatenate([mix_beyond, jnp.zeros((6, LANES), F32)], axis=0)
            result = (
                taps[i : i + 1, at] * ext[0:rows]
                + taps[3 + i : 4 + i, at] * ext[1 : rows + 1]
                + taps[6 + i : 7 + i, at] * ext[2 : rows + 2]
            )
            out[i, :, at] = result.astype(BF)

        ext[0:HEAD] = gate_head[:, at].astype(F32)
        ext[HEAD:rows] = gate_tail[:, at].astype(F32)
        finish(0, rim_f[1:3])
        for i, stream, mix_beyond in streams:
            ext[0:LANES] = (picked[:, :LANES] * stream[0:LANES, at]).astype(BF).astype(F32)
            ext[LANES : 2 * LANES] = (
                (picked[:, LANES:] * stream[LANES : 2 * LANES, at]).astype(BF).astype(F32)
            )
            finish(i, mix_beyond)
        return carry

    lax.fori_loop(0, key.shape[1] // LANES, tile, 0)


def final_part(convs, gates, halo, key, value, feats, taps, back):
    rows, channels = key.shape
    return pl.pallas_call(
        final_kernel,
        out_shape=jax.ShapeDtypeStruct((3, rows, channels), BF),
        in_specs=vmem(10),
        out_specs=vmem(1)[0],
        scratch_shapes=[pltpu.VMEM((rows + 8, LANES), F32), pltpu.VMEM((16, LANES), F32)],
        compiler_params=params(8),
        cost_estimate=pl.CostEstimate(flops=2 << 30, bytes_accessed=12 << 20, transcendentals=0),
        name="final_part",
    )(*convs, *gates, halo, key, value, feats, taps, back)


def spread(quarters):
    flat = quarters.reshape((X * RING // 2,) + quarters.shape[2:])
    return lax.all_to_all(flat, ("x", "yq"), 0, 0).reshape(quarters.shape)


def local(features, short_taps, long_filters, out_weight, out_grad):
    feats = jnp.transpose(features[0], (1, 0, 2))
    _, channels = feats.shape[1:]
    taps = short_taps[0].reshape(9, channels)
    filters = jnp.transpose(long_filters[0])

    quarters = quarters_of(out_grad[0])
    weight = out_weight[0]
    b_held = gather_ring([weight[: channels // 2], weight[channels // 2 :]], "z")
    mine = spread(quarters)
    even = pair_ring(mine[: X // 2], ("yq", "yb"), 0)
    odd = pair_ring(mine[X // 2 :], ("yq", "yb"), 1)
    a_held = (mine, even, odd)
    halo_before = shift_ctx(tail_rows(feats, taps), 1, 1)
    feats = swap(feats)
    taps = swap(taps)
    filters = swap(filters)
    conv, gate, key, value, back = forward_part(feats, taps, filters, halo_before)

    send_head, keep_head, a_tail, b_full = head_products(a_held, b_held)
    got_head = pair_x(send_head, 1, 0)
    send_tail, keep_tail = tail_products(a_tail, b_full)
    got_tail = pair_x(send_tail, 3, 0)
    head, tail, own = fold(keep_head, got_head, keep_tail, got_tail)
    last_head = pair_x(head, 3, 1)
    last_tail = pair_x(tail, 1, 1)
    own = swap(own)
    conv_head, cross_head, halo = gate_head(own, last_head, conv, gate, feats)
    conv_tail, cross_tail = gate_tail(own, last_tail, conv, gate)
    halo_after = shift_ctx(halo, -1, 0)
    grad_feat = final_part(
        (conv_head, conv_tail), (cross_head, cross_tail), halo_after, key, value, feats, taps, back
    )
    return jnp.transpose(grad_feat, (1, 0, 2))[None]


def solution(mesh):
    parts = jax.sharding.Mesh(
        mesh.devices.reshape(RING, X, RING // 2, 2, 2),
        ("z", "x", "yq", "yb", "pp"),
        axis_types=(jax.sharding.AxisType.Auto,) * 5,
    )
    ctx, tp = ("z", "x"), ("yq", "yb")
    in_specs = (
        P("pp", ctx, None, tp),
        P("pp", None, None, tp),
        P("pp", None, tp),
        P("pp", tp, ctx),
        P("pp", ctx, tp),
    )
    out_specs = P("pp", ctx, None, tp)

    return jax.shard_map(local, mesh=parts, in_specs=in_specs, out_specs=out_specs, check_vma=False)
```

```python
import jax
import jax.numpy as jnp
from jax import lax
from jax.experimental import pallas as pl
from jax.experimental.pallas import tpu as pltpu
from jax.sharding import PartitionSpec as P

BF = jnp.bfloat16
F32 = jnp.float32
LANES = 128
X = 4
RING = 8
HALO = 144
HEAD = 144


def vmem(n):
    return [pl.BlockSpec(memory_space=pltpu.VMEM)] * n


def params(mib):
    return pltpu.CompilerParams(vmem_limit_bytes=mib << 20)


def partner(i, parity):
    return (i + 1) % RING if i % 2 == parity else (i - 1) % RING


def pair_ring(v, axis, parity):
    return lax.ppermute(v, axis, [(i, partner(i, parity)) for i in range(RING)])


def pair_x(v, flip, cross):
    route = [(x * 2 + p, (x ^ flip) * 2 + (p ^ cross)) for x in range(X) for p in range(2)]
    return lax.ppermute(v, ("x", "pp"), route)


def swap(v):
    return lax.ppermute(v, "pp", [(0, 1), (1, 0)])


def shift_ctx(v, by, cross):
    n = RING * X
    route = []
    for i in range(n):
        for p in range(2):
            if 0 <= i + by < n:
                route.append((i * 2 + p, (i + by) * 2 + (p ^ cross)))
    return lax.ppermute(v, ("z", "x", "pp"), route)


def join_kernel(own, first, out):
    out[0] = own[...]
    out[1] = first[...]


def join(own, first):
    return pl.pallas_call(
        join_kernel,
        out_shape=jax.ShapeDtypeStruct((2,) + own.shape, BF),
        in_specs=vmem(2),
        out_specs=vmem(1)[0],
        compiler_params=params(2),
        cost_estimate=pl.CostEstimate(flops=1 << 10, bytes_accessed=1 << 18, transcendentals=0),
        name="join",
    )(own, first)


def gather_ring(halves, axis):
    def hop(n, turn, v):
        return pair_ring(v, axis, (n + turn) % 2)

    firsts = [hop(n, 0, halves[n]) for n in range(2)]
    held = [[join(halves[n], firsts[n]) for n in range(2)]]
    for turn in (1, 2, 3):
        now = lax.optimization_barrier(held[-1])
        held.append([hop(n, turn, now[n]) for n in range(2)])
    return held


def place_rows(mine, even, odd, head, tail):
    x, side = lax.axis_index("x"), lax.axis_index("yb")
    rest = mine.shape[2] - HEAD

    def put(value, slot, y):
        at = pl.ds(pl.multiple_of(y * LANES, LANES), LANES)
        head[pl.ds(pl.multiple_of(slot * HEAD, 16), HEAD), at] = value[:HEAD]
        tail[pl.ds(pl.multiple_of(slot * rest, 16), rest), at] = value[HEAD:]

    for m in range(X):
        slot = jnp.bitwise_xor(m, x)
        there = even[m] if m < X // 2 else odd[m - X // 2]
        for k in range(RING // 2):
            put(mine[m, k], slot, 2 * k + side)
            put(there[k], slot, 2 * k + 1 - side)


def place(held, full_ref, me):
    rows = full_ref.shape[0] // 2
    for n in range(2):
        step = jnp.where(lax.rem(me, 2) == n, 1, -1)
        spots = [(0, step), (-step, -2 * step), (2 * step, 3 * step), (-3 * step, -4 * step)]
        for turn in range(4):
            for k in range(2):
                index = lax.rem(me + spots[turn][k] + 2 * RING, RING)
                at = pl.multiple_of(index * LANES, LANES)
                full_ref[n * rows : (n + 1) * rows, pl.ds(at, LANES)] = held[turn * 2 + n][k]


def multiply(rows_ref, slots, b_full, store):
    size = rows_ref.shape[0] // X
    first, count = slots
    width = 2 * LANES

    def columns(c, carry):
        at = pl.ds(pl.multiple_of(c * width, width), width)
        product = lax.dot_general(
            rows_ref[first * size : (first + count) * size, :],
            b_full[at, :],
            (((1,), (1,)), ((), ())),
            preferred_element_type=F32,
        )
        store(at, *[product[n * size : (n + 1) * size] for n in range(count)])
        return carry

    lax.fori_loop(0, b_full.shape[0] // width, columns, 0)


def head_send_kernel(*refs):
    a_held, b_held, (send, a_head, a_tail, b_full) = refs[:3], refs[3:11], refs[11:]
    place_rows(*a_held, a_head, a_tail)
    place(b_held, b_full, lax.axis_index("z"))

    def store(at, near, across):
        send[0, :, at] = near.astype(BF)
        send[1, :, at] = across.astype(BF)

    multiply(a_head, (1, 2), b_full, store)


def tail_send_kernel(a_tail, b_full, send):
    def store(at, across, far):
        send[0, :, at] = far.astype(BF)
        send[1, :, at] = across.astype(BF)

    multiply(a_tail, (2, 2), b_full, store)


def keep_kernel(a_head, a_tail, b_full, keep_head, keep_tail):
    def one(ref, spot):
        def store(at, part):
            ref[spot, :, at] = part

        return store

    def two(at, own, near):
        keep_tail[0, :, at] = own
        keep_tail[1, :, at] = near

    multiply(a_head, (0, 1), b_full, one(keep_head, 0))
    multiply(a_head, (3, 1), b_full, one(keep_head, 1))
    multiply(a_tail, (0, 2), b_full, two)


def product_call(kernel, outs, flops, *args):
    return pl.pallas_call(
        kernel,
        out_shape=[jax.ShapeDtypeStruct(shape, dtype) for shape, dtype in outs],
        in_specs=vmem(len(args)),
        out_specs=vmem(len(outs)),
        compiler_params=params(8),
        cost_estimate=pl.CostEstimate(flops=flops, bytes_accessed=6 << 20, transcendentals=0),
    )(*args)


def head_send(a_held, b_held):
    b_list = [v for parts in b_held for v in parts]
    rest = a_held[0].shape[2] - HEAD
    cols = 2 * b_list[0].shape[1]
    depth = RING * LANES
    outs = (
        ((2, HEAD, cols), BF),
        ((X * HEAD, depth), BF),
        ((X * rest, depth), BF),
        ((cols, depth), BF),
    )
    return product_call(head_send_kernel, outs, 1 << 29, *a_held, *b_list)


def tail_send(a_tail, b_full):
    outs = (((2, a_tail.shape[0] // X, b_full.shape[0]), BF),)
    return product_call(tail_send_kernel, outs, 1 << 29, a_tail, b_full)[0]


def kept(a_head, a_tail, b_full):
    cols = b_full.shape[0]
    outs = [((2, rows.shape[0] // X, cols), F32) for rows in (a_head, a_tail)]
    return product_call(keep_kernel, outs, 1 << 30, a_head, a_tail, b_full)


def fold_kernel(keep_head, got_head, keep_tail, got_tail, out_head, out_tail, own):
    out_head[...] = (keep_head[1] + got_head[1].astype(F32)).astype(BF)
    out_tail[...] = (keep_tail[1] + got_tail[1].astype(F32)).astype(BF)
    own[0:HEAD] = (keep_head[0] + got_head[0].astype(F32)).astype(BF)
    own[HEAD:] = (keep_tail[0] + got_tail[0].astype(F32)).astype(BF)


def fold(keep_head, got_head, keep_tail, got_tail):
    head, tail = got_head.shape[1:], got_tail.shape[1:]
    return pl.pallas_call(
        fold_kernel,
        out_shape=[
            jax.ShapeDtypeStruct(head, BF),
            jax.ShapeDtypeStruct(tail, BF),
            jax.ShapeDtypeStruct((head[0] + tail[0], head[1]), BF),
        ],
        in_specs=vmem(4),
        out_specs=vmem(3),
        compiler_params=params(2),
        cost_estimate=pl.CostEstimate(flops=1 << 18, bytes_accessed=4 << 20, transcendentals=0),
        name="fold",
    )(keep_head, got_head, keep_tail, got_tail)


def quarter_kernel(cotangent, out):
    for x in range(X):
        quarter = cotangent[:, x * LANES : (x + 1) * LANES]
        for k in range(RING // 2):
            out[x, k] = quarter


def quarters_of(cotangent):
    return pl.pallas_call(
        quarter_kernel,
        out_shape=jax.ShapeDtypeStruct((X, RING // 2, cotangent.shape[0], LANES), BF),
        in_specs=vmem(1),
        out_specs=vmem(1)[0],
        compiler_params=params(2),
        cost_estimate=pl.CostEstimate(flops=1 << 10, bytes_accessed=1 << 20, transcendentals=0),
        name="quarters",
    )(cotangent)


def lane_tile(index):
    return pl.ds(pl.multiple_of(index * LANES, LANES), LANES)


def tail_kernel(feats, taps, out, ext):
    rows = feats.shape[1]
    keep = rows - LANES

    def tile(l, carry):
        at = lane_tile(l)
        mixed = []
        for i in (1, 2):
            ext[...] = feats[i, keep - 16 : rows, at].astype(F32)
            mixed.append(
                taps[i : i + 1, at] * ext[16 : 16 + LANES]
                + taps[3 + i : 4 + i, at] * ext[15 : 15 + LANES]
                + taps[6 + i : 7 + i, at] * ext[14 : 14 + LANES]
            )
        out[0:LANES, at] = (mixed[0] * mixed[1]).astype(BF)
        last = [feats[i, rows - 16 : rows, at].astype(F32)[14:16] for i in range(3)]
        last.append(jnp.zeros((10, LANES), F32))
        out[LANES:HALO, at] = jnp.concatenate(last, axis=0).astype(BF)
        return carry

    lax.fori_loop(0, feats.shape[2] // LANES, tile, 0)


def tail_rows(feats, taps):
    channels = feats.shape[2]
    return pl.pallas_call(
        tail_kernel,
        out_shape=jax.ShapeDtypeStruct((HALO, channels), BF),
        in_specs=vmem(2),
        out_specs=vmem(1)[0],
        scratch_shapes=[pltpu.VMEM((LANES + 16, LANES), F32)],
        compiler_params=params(8),
        cost_estimate=pl.CostEstimate(flops=1 << 20, bytes_accessed=2 << 20, transcendentals=0),
        name="tail_rows",
    )(feats, taps)


def pick_groups(product, per_tile, width):
    rows = product.shape[0] // per_tile
    shape = (rows, product.shape[1])
    group = lax.rem(lax.broadcasted_iota(jnp.int32, shape, 1), LANES) // width
    out = product[:rows]
    for g in range(1, per_tile):
        out = jnp.where(group == g, product[g * rows : (g + 1) * rows], out)
    return out


def forward_kernel(feats, taps, filters, halo, conv, gate, key, value, back, fwd_band, flipped, plain, ext):
    rows = feats.shape[1]
    groups = filters.shape[0]
    per_tile = groups * LANES // feats.shape[2]
    width = LANES // per_tile
    row = lax.broadcasted_iota(jnp.int32, (LANES, LANES), 0)
    col = lax.broadcasted_iota(jnp.int32, (LANES, LANES), 1)
    mirror = jnp.where(lax.rem(row + col, LANES) == 0, 1.0, 0.0).astype(BF)
    flipped[...] = jnp.dot(filters[...], mirror, preferred_element_type=F32)
    plain[...] = filters[...].astype(F32)

    def tile(l, carry):
        at = lane_tile(l)
        for g in range(per_tile):
            index = l * per_tile + g
            spread = jnp.broadcast_to(plain[pl.ds(index, 1), :], (LANES, LANES))
            turned = pltpu.roll(spread, 0, 1, stride=1, stride_axis=0)
            back[index, :, 0:LANES] = jnp.where(col >= row, turned, 0.0).astype(BF)
            back[index, :, LANES : 2 * LANES] = jnp.where(col < row, turned, 0.0).astype(BF)
            spread = jnp.broadcast_to(flipped[pl.ds(index, 1), :], (LANES, LANES))
            turned = pltpu.roll(spread, 0, 1, stride=1, stride_axis=0)
            fwd_band[g * LANES : (g + 1) * LANES, 0:LANES] = jnp.where(col > row, turned, 0.0).astype(BF)
            fwd_band[g * LANES : (g + 1) * LANES, LANES : 2 * LANES] = jnp.where(
                col <= row, turned, 0.0
            ).astype(BF)
        before = halo[LANES:HALO, at].astype(F32)
        mixed = []
        for i in range(3):
            ext[0:8] = jnp.concatenate([jnp.zeros((6, LANES), F32), before[2 * i : 2 * i + 2]], axis=0)
            ext[8 : 8 + rows] = feats[i, :, at].astype(F32)
            mixed.append(
                taps[i : i + 1, at] * ext[8 : 8 + rows]
                + taps[3 + i : 4 + i, at] * ext[7 : 7 + rows]
                + taps[6 + i : 7 + i, at] * ext[6 : 6 + rows]
            )
        gate[:, at] = mixed[0]
        key[:, at] = mixed[1]
        value[:, at] = mixed[2]
        products = (mixed[1] * mixed[2]).astype(BF)
        first = jnp.concatenate([halo[0:LANES, at], products[:LANES]], axis=0)
        window = jnp.concatenate([first, products], axis=1)
        picked = pick_groups(
            jnp.dot(fwd_band[...], window, preferred_element_type=F32), per_tile, width
        )
        conv[0:LANES, at] = picked[:, :LANES]
        conv[LANES : 2 * LANES, at] = picked[:, LANES:]
        return carry

    lax.fori_loop(0, feats.shape[2] // LANES, tile, 0)


def forward_part(feats, taps, filters, halo):
    _, rows, channels = feats.shape
    groups = filters.shape[0]
    full = jax.ShapeDtypeStruct((rows, channels), F32)
    per_tile = groups * LANES // channels
    return pl.pallas_call(
        forward_kernel,
        out_shape=[full] * 4 + [jax.ShapeDtypeStruct((groups, LANES, 2 * LANES), BF)],
        in_specs=vmem(4),
        out_specs=vmem(5),
        scratch_shapes=[
            pltpu.VMEM((per_tile * LANES, 2 * LANES), BF),
            pltpu.VMEM((groups, LANES), F32),
            pltpu.VMEM((groups, LANES), F32),
            pltpu.VMEM((rows + 8, LANES), F32),
        ],
        compiler_params=params(8),
        cost_estimate=pl.CostEstimate(flops=2 << 30, bytes_accessed=12 << 20, transcendentals=0),
        name="forward_part",
    )(feats, taps, filters, halo)


def gated(own, last, conv, gate, grad_conv, grad_gate):
    grad_y = (own.astype(F32) + last[...].astype(F32)).astype(BF).astype(F32)
    down = (grad_y * gate).astype(BF)
    across = (grad_y * conv).astype(BF)
    grad_conv[...] = down
    grad_gate[...] = across
    return down, across


def head_kernel(own, last, conv, gate, feats, grad_conv, grad_gate, halo):
    down, across = gated(own[0:HEAD], last, conv[0:HEAD], gate[0:HEAD], grad_conv, grad_gate)
    halo[0:LANES] = down[0:LANES]
    pieces = [
        down[LANES:HEAD].astype(F32)[0:1],
        across[0:16].astype(F32)[0:2],
        feats[1, 0:16].astype(F32)[0:2],
        feats[2, 0:16].astype(F32)[0:2],
        jnp.zeros((9, down.shape[1]), F32),
    ]
    halo[LANES:HALO] = jnp.concatenate(pieces, axis=0).astype(BF)


def tail_gate_kernel(own, last, conv, gate, grad_conv, grad_gate):
    rows = conv.shape[0]
    gated(own[HEAD:rows], last, conv[HEAD:rows], gate[HEAD:rows], grad_conv, grad_gate)


def gate_head(own, last, conv, gate, feats):
    half = jax.ShapeDtypeStruct(last.shape, BF)
    return pl.pallas_call(
        head_kernel,
        out_shape=[half, half, jax.ShapeDtypeStruct((HALO, last.shape[1]), BF)],
        in_specs=vmem(5),
        out_specs=vmem(3),
        compiler_params=params(8),
        cost_estimate=pl.CostEstimate(flops=1 << 20, bytes_accessed=3 << 20, transcendentals=0),
        name="gate_head",
    )(own, last, conv, gate, feats)


def gate_tail(own, last, conv, gate):
    half = jax.ShapeDtypeStruct(last.shape, BF)
    return pl.pallas_call(
        tail_gate_kernel,
        out_shape=[half, half],
        in_specs=vmem(4),
        out_specs=vmem(2),
        compiler_params=params(8),
        cost_estimate=pl.CostEstimate(flops=1 << 20, bytes_accessed=3 << 20, transcendentals=0),
        name="gate_tail",
    )(own, last, conv, gate)


def final_kernel(
    conv_head, conv_tail, gate_head, gate_tail, halo, key, value, feats, taps, back,
    out, ext, small, done, sems
):
    rows = key.shape[0]
    groups = back.shape[0]
    per_tile = groups * LANES // key.shape[1]
    width = LANES // per_tile

    def leave(l, slot):
        return pltpu.make_async_copy(done.at[slot], out.at[:, :, lane_tile(l)], sems.at[slot])

    def tile(l, carry):
        at = lane_tile(l)
        slot = lax.rem(l, 2)

        @pl.when(l >= 2)
        def _():
            leave(l - 2, slot).wait()

        mine = jnp.concatenate([conv_head[:, at], conv_tail[:, at]], axis=0)
        after = halo[0:LANES, at]
        second = jnp.concatenate([mine[LANES:], after], axis=0)
        window = jnp.concatenate([mine, second], axis=1)
        first_group = pl.multiple_of(l * per_tile, per_tile)
        band = back[pl.ds(first_group, per_tile)]
        picked = pick_groups(
            jnp.dot(
                band.reshape(per_tile * LANES, 2 * LANES), window, preferred_element_type=F32
            ),
            per_tile,
            width,
        )
        rim = halo[LANES:HALO, at]
        beyond = jnp.concatenate([after, rim, jnp.zeros((LANES - 16, LANES), BF)], axis=0)
        top = band[:, 0:16, :].reshape(per_tile * 16, 2 * LANES)
        extra = pick_groups(jnp.dot(top, beyond, preferred_element_type=F32), per_tile, width)[0:2]
        rim_f = rim.astype(F32)
        streams = []
        for i, stream in ((1, value), (2, key)):
            other = 3 - i
            small[0:8] = feats[other, rows - 16 : rows, at].astype(F32)[8:16]
            small[8:16] = jnp.concatenate(
                [rim_f[1 + 2 * other : 3 + 2 * other], jnp.zeros((6, LANES), F32)], axis=0
            )
            beyond_mixed = (
                taps[other : other + 1, at] * small[8:10]
                + taps[3 + other : 4 + other, at] * small[7:9]
                + taps[6 + other : 7 + other, at] * small[6:8]
            )
            streams.append((i, stream, (extra * beyond_mixed).astype(BF).astype(F32)))

        def finish(i, mix_beyond):
            ext[rows : rows + 8] = jnp.concatenate([mix_beyond, jnp.zeros((6, LANES), F32)], axis=0)
            result = (
                taps[i : i + 1, at] * ext[0:rows]
                + taps[3 + i : 4 + i, at] * ext[1 : rows + 1]
                + taps[6 + i : 7 + i, at] * ext[2 : rows + 2]
            )
            done[slot, i] = result.astype(BF)

        ext[0:HEAD] = gate_head[:, at].astype(F32)
        ext[HEAD:rows] = gate_tail[:, at].astype(F32)
        finish(0, rim_f[1:3])
        for i, stream, mix_beyond in streams:
            ext[0:LANES] = (picked[:, :LANES] * stream[0:LANES, at]).astype(BF).astype(F32)
            ext[LANES : 2 * LANES] = (
                (picked[:, LANES:] * stream[LANES : 2 * LANES, at]).astype(BF).astype(F32)
            )
            finish(i, mix_beyond)
        leave(l, slot).start()
        return carry

    tiles = key.shape[1] // LANES
    lax.fori_loop(0, tiles, tile, 0)
    for l in (tiles - 2, tiles - 1):
        leave(l, l % 2).wait()


def final_part(convs, gates, halo, key, value, feats, taps, back):
    rows, channels = key.shape
    return pl.pallas_call(
        final_kernel,
        out_shape=jax.ShapeDtypeStruct((3, rows, channels), BF),
        in_specs=vmem(10),
        out_specs=pl.BlockSpec(memory_space=pl.ANY),
        scratch_shapes=[
            pltpu.VMEM((rows + 8, LANES), F32),
            pltpu.VMEM((16, LANES), F32),
            pltpu.VMEM((2, 3, rows, LANES), BF),
            pltpu.SemaphoreType.DMA((2,)),
        ],
        compiler_params=params(8),
        cost_estimate=pl.CostEstimate(flops=2 << 30, bytes_accessed=12 << 20, transcendentals=0),
        name="final_part",
    )(*convs, *gates, halo, key, value, feats, taps, back)


def spread(quarters):
    flat = quarters.reshape((X * RING // 2,) + quarters.shape[2:])
    return lax.all_to_all(flat, ("x", "yq"), 0, 0).reshape(quarters.shape)


def local(features, short_taps, long_filters, out_weight, out_grad):
    feats = jnp.transpose(features[0], (1, 0, 2))
    _, channels = feats.shape[1:]
    taps = short_taps[0].reshape(9, channels)
    filters = jnp.transpose(long_filters[0])

    quarters = quarters_of(out_grad[0])
    weight = out_weight[0]
    b_held = gather_ring([weight[: channels // 2], weight[channels // 2 :]], "z")
    mine = spread(quarters)
    even = pair_ring(mine[: X // 2], ("yq", "yb"), 0)
    odd = pair_ring(mine[X // 2 :], ("yq", "yb"), 1)
    a_held = (mine, even, odd)
    halo_before = shift_ctx(tail_rows(feats, taps), 1, 1)
    feats = swap(feats)
    taps = swap(taps)
    filters = swap(filters)
    conv, gate, key, value, back = forward_part(feats, taps, filters, halo_before)

    send_head, a_head, a_tail, b_full = head_send(a_held, b_held)
    got_head = pair_x(send_head, 1, 0)
    send_tail = tail_send(a_tail, b_full)
    keep_head, keep_tail = kept(a_head, a_tail, b_full)
    got_tail = pair_x(send_tail, 3, 0)
    head, tail, own = fold(keep_head, got_head, keep_tail, got_tail)
    last_head = pair_x(head, 3, 1)
    last_tail = pair_x(tail, 1, 1)
    own = swap(own)
    conv_head, cross_head, halo = gate_head(own, last_head, conv, gate, feats)
    conv_tail, cross_tail = gate_tail(own, last_tail, conv, gate)
    halo_after = shift_ctx(halo, -1, 0)
    grad_feat = final_part(
        (conv_head, conv_tail), (cross_head, cross_tail), halo_after, key, value, feats, taps, back
    )
    return jnp.transpose(grad_feat, (1, 0, 2))[None]


def solution(mesh):
    parts = jax.sharding.Mesh(
        mesh.devices.reshape(RING, X, RING // 2, 2, 2),
        ("z", "x", "yq", "yb", "pp"),
        axis_types=(jax.sharding.AxisType.Auto,) * 5,
    )
    ctx, tp = ("z", "x"), ("yq", "yb")
    in_specs = (
        P("pp", ctx, None, tp),
        P("pp", None, None, tp),
        P("pp", None, tp),
        P("pp", tp, ctx),
        P("pp", ctx, tp),
    )
    out_specs = P("pp", ctx, None, tp)

    return jax.shard_map(local, mesh=parts, in_specs=in_specs, out_specs=out_specs, check_vma=False)
```

```python
import jax
import jax.numpy as jnp
from jax import lax
from jax.experimental import pallas as pl
from jax.experimental.pallas import tpu as pltpu
from jax.sharding import PartitionSpec as P

BF = jnp.bfloat16
F32 = jnp.float32
LANES = 128
X = 4
RING = 8
HALO = 144
HEAD = 144


def vmem(n):
    return [pl.BlockSpec(memory_space=pltpu.VMEM)] * n


def params(mib):
    return pltpu.CompilerParams(vmem_limit_bytes=mib << 20)


def partner(i, parity):
    return (i + 1) % RING if i % 2 == parity else (i - 1) % RING


def pair_ring(v, axis, parity):
    return lax.ppermute(v, axis, [(i, partner(i, parity)) for i in range(RING)])


def pair_x(v, flip, cross):
    route = [(x * 2 + p, (x ^ flip) * 2 + (p ^ cross)) for x in range(X) for p in range(2)]
    return lax.ppermute(v, ("x", "pp"), route)


def swap(v):
    return lax.ppermute(v, "pp", [(0, 1), (1, 0)])


def shift_ctx(v, by, cross):
    n = RING * X
    route = []
    for i in range(n):
        for p in range(2):
            if 0 <= i + by < n:
                route.append((i * 2 + p, (i + by) * 2 + (p ^ cross)))
    return lax.ppermute(v, ("z", "x", "pp"), route)


def join_kernel(own, first, out):
    out[0] = own[...]
    out[1] = first[...]


def join(own, first):
    return pl.pallas_call(
        join_kernel,
        out_shape=jax.ShapeDtypeStruct((2,) + own.shape, BF),
        in_specs=vmem(2),
        out_specs=vmem(1)[0],
        compiler_params=params(2),
        cost_estimate=pl.CostEstimate(flops=1 << 10, bytes_accessed=1 << 18, transcendentals=0),
        name="join",
    )(own, first)


def gather_ring(halves, axis):
    def hop(n, turn, v):
        return pair_ring(v, axis, (n + turn) % 2)

    firsts = [hop(n, 0, halves[n]) for n in range(2)]
    held = [[join(halves[n], firsts[n]) for n in range(2)]]
    for turn in (1, 2, 3):
        now = lax.optimization_barrier(held[-1])
        held.append([hop(n, turn, now[n]) for n in range(2)])
    return held


def place_rows(mine, even, odd, head, tail):
    x, side = lax.axis_index("x"), lax.axis_index("yb")
    rest = mine.shape[2] - HEAD

    def put(value, slot, y):
        at = pl.ds(pl.multiple_of(y * LANES, LANES), LANES)
        head[pl.ds(pl.multiple_of(slot * HEAD, 16), HEAD), at] = value[:HEAD]
        tail[pl.ds(pl.multiple_of(slot * rest, 16), rest), at] = value[HEAD:]

    for m in range(X):
        slot = jnp.bitwise_xor(m, x)
        there = even[m] if m < X // 2 else odd[m - X // 2]
        for k in range(RING // 2):
            put(mine[m, k], slot, 2 * k + side)
            put(there[k], slot, 2 * k + 1 - side)


def place(held, full_ref, me):
    rows = full_ref.shape[0] // 2
    for n in range(2):
        step = jnp.where(lax.rem(me, 2) == n, 1, -1)
        spots = [(0, step), (-step, -2 * step), (2 * step, 3 * step), (-3 * step, -4 * step)]
        for turn in range(4):
            for k in range(2):
                index = lax.rem(me + spots[turn][k] + 2 * RING, RING)
                at = pl.multiple_of(index * LANES, LANES)
                full_ref[n * rows : (n + 1) * rows, pl.ds(at, LANES)] = held[turn * 2 + n][k]


def multiply(rows_ref, slots, b_full, store):
    size = rows_ref.shape[0] // X
    first, count = slots
    width = 2 * LANES

    def columns(c, carry):
        at = pl.ds(pl.multiple_of(c * width, width), width)
        product = lax.dot_general(
            rows_ref[first * size : (first + count) * size, :],
            b_full[at, :],
            (((1,), (1,)), ((), ())),
            preferred_element_type=F32,
        )
        store(at, *[product[n * size : (n + 1) * size] for n in range(count)])
        return carry

    lax.fori_loop(0, b_full.shape[0] // width, columns, 0)


def head_send_kernel(*refs):
    a_held, b_held, (send, a_head, a_tail, b_full) = refs[:3], refs[3:11], refs[11:]
    place_rows(*a_held, a_head, a_tail)
    place(b_held, b_full, lax.axis_index("z"))

    def store(at, near, across):
        send[0, :, at] = near.astype(BF)
        send[1, :, at] = across.astype(BF)

    multiply(a_head, (1, 2), b_full, store)


def tail_send_kernel(a_tail, b_full, send):
    def store(at, across, far):
        send[0, :, at] = far.astype(BF)
        send[1, :, at] = across.astype(BF)

    multiply(a_tail, (2, 2), b_full, store)


def keep_kernel(a_head, a_tail, b_full, keep_head, keep_tail):
    def one(ref, spot):
        def store(at, part):
            ref[spot, :, at] = part

        return store

    def two(at, own, near):
        keep_tail[0, :, at] = own
        keep_tail[1, :, at] = near

    multiply(a_head, (0, 1), b_full, one(keep_head, 0))
    multiply(a_head, (3, 1), b_full, one(keep_head, 1))
    multiply(a_tail, (0, 2), b_full, two)


def product_call(kernel, outs, flops, *args):
    return pl.pallas_call(
        kernel,
        out_shape=[jax.ShapeDtypeStruct(shape, dtype) for shape, dtype in outs],
        in_specs=vmem(len(args)),
        out_specs=vmem(len(outs)),
        compiler_params=params(8),
        cost_estimate=pl.CostEstimate(flops=flops, bytes_accessed=6 << 20, transcendentals=0),
    )(*args)


def head_send(a_held, b_held):
    b_list = [v for parts in b_held for v in parts]
    rest = a_held[0].shape[2] - HEAD
    cols = 2 * b_list[0].shape[1]
    depth = RING * LANES
    outs = (
        ((2, HEAD, cols), BF),
        ((X * HEAD, depth), BF),
        ((X * rest, depth), BF),
        ((cols, depth), BF),
    )
    return product_call(head_send_kernel, outs, 1 << 29, *a_held, *b_list)


def tail_send(a_tail, b_full):
    outs = (((2, a_tail.shape[0] // X, b_full.shape[0]), BF),)
    return product_call(tail_send_kernel, outs, 1 << 29, a_tail, b_full)[0]


def kept(a_head, a_tail, b_full):
    cols = b_full.shape[0]
    outs = [((2, rows.shape[0] // X, cols), F32) for rows in (a_head, a_tail)]
    return product_call(keep_kernel, outs, 1 << 30, a_head, a_tail, b_full)


def fold_kernel(keep_head, got_head, keep_tail, got_tail, out_head, out_tail, own):
    out_head[...] = (keep_head[1] + got_head[1].astype(F32)).astype(BF)
    out_tail[...] = (keep_tail[1] + got_tail[1].astype(F32)).astype(BF)
    own[0:HEAD] = (keep_head[0] + got_head[0].astype(F32)).astype(BF)
    own[HEAD:] = (keep_tail[0] + got_tail[0].astype(F32)).astype(BF)


def fold(keep_head, got_head, keep_tail, got_tail):
    head, tail = got_head.shape[1:], got_tail.shape[1:]
    return pl.pallas_call(
        fold_kernel,
        out_shape=[
            jax.ShapeDtypeStruct(head, BF),
            jax.ShapeDtypeStruct(tail, BF),
            jax.ShapeDtypeStruct((head[0] + tail[0], head[1]), BF),
        ],
        in_specs=vmem(4),
        out_specs=vmem(3),
        compiler_params=params(2),
        cost_estimate=pl.CostEstimate(flops=1 << 18, bytes_accessed=4 << 20, transcendentals=0),
        name="fold",
    )(keep_head, got_head, keep_tail, got_tail)


def quarter_kernel(cotangent, out):
    for x in range(X):
        quarter = cotangent[:, x * LANES : (x + 1) * LANES]
        for k in range(RING // 2):
            out[x, k] = quarter


def quarters_of(cotangent):
    return pl.pallas_call(
        quarter_kernel,
        out_shape=jax.ShapeDtypeStruct((X, RING // 2, cotangent.shape[0], LANES), BF),
        in_specs=vmem(1),
        out_specs=vmem(1)[0],
        compiler_params=params(2),
        cost_estimate=pl.CostEstimate(flops=1 << 10, bytes_accessed=1 << 20, transcendentals=0),
        name="quarters",
    )(cotangent)


def lane_tile(index):
    return pl.ds(pl.multiple_of(index * LANES, LANES), LANES)


def tail_kernel(feats, taps, out, ext):
    rows = feats.shape[1]
    keep = rows - LANES

    def tile(l, carry):
        at = lane_tile(l)
        mixed = []
        for i in (1, 2):
            ext[...] = feats[i, keep - 16 : rows, at].astype(F32)
            mixed.append(
                taps[i : i + 1, at] * ext[16 : 16 + LANES]
                + taps[3 + i : 4 + i, at] * ext[15 : 15 + LANES]
                + taps[6 + i : 7 + i, at] * ext[14 : 14 + LANES]
            )
        out[0:LANES, at] = (mixed[0] * mixed[1]).astype(BF)
        last = [feats[i, rows - 16 : rows, at].astype(F32)[14:16] for i in range(3)]
        last.append(jnp.zeros((10, LANES), F32))
        out[LANES:HALO, at] = jnp.concatenate(last, axis=0).astype(BF)
        return carry

    lax.fori_loop(0, feats.shape[2] // LANES, tile, 0)


def tail_rows(feats, taps):
    channels = feats.shape[2]
    return pl.pallas_call(
        tail_kernel,
        out_shape=jax.ShapeDtypeStruct((HALO, channels), BF),
        in_specs=vmem(2),
        out_specs=vmem(1)[0],
        scratch_shapes=[pltpu.VMEM((LANES + 16, LANES), F32)],
        compiler_params=params(8),
        cost_estimate=pl.CostEstimate(flops=1 << 20, bytes_accessed=2 << 20, transcendentals=0),
        name="tail_rows",
    )(feats, taps)


def pick_groups(product, per_tile, width):
    rows = product.shape[0] // per_tile
    shape = (rows, product.shape[1])
    group = lax.rem(lax.broadcasted_iota(jnp.int32, shape, 1), LANES) // width
    out = product[:rows]
    for g in range(1, per_tile):
        out = jnp.where(group == g, product[g * rows : (g + 1) * rows], out)
    return out


def forward_kernel(feats, taps, filters, halo, conv, gate, key, value, back, fwd_band, flipped, plain, ext):
    rows = feats.shape[1]
    groups = filters.shape[0]
    per_tile = groups * LANES // feats.shape[2]
    width = LANES // per_tile
    row = lax.broadcasted_iota(jnp.int32, (LANES, LANES), 0)
    col = lax.broadcasted_iota(jnp.int32, (LANES, LANES), 1)
    mirror = jnp.where(lax.rem(row + col, LANES) == 0, 1.0, 0.0).astype(BF)
    flipped[...] = jnp.dot(filters[...], mirror, preferred_element_type=F32)
    plain[...] = filters[...].astype(F32)

    def tile(l, carry):
        at = lane_tile(l)
        for g in range(per_tile):
            index = l * per_tile + g
            spread = jnp.broadcast_to(plain[pl.ds(index, 1), :], (LANES, LANES))
            turned = pltpu.roll(spread, 0, 1, stride=1, stride_axis=0)
            back[index, :, 0:LANES] = jnp.where(col >= row, turned, 0.0).astype(BF)
            back[index, :, LANES : 2 * LANES] = jnp.where(col < row, turned, 0.0).astype(BF)
            spread = jnp.broadcast_to(flipped[pl.ds(index, 1), :], (LANES, LANES))
            turned = pltpu.roll(spread, 0, 1, stride=1, stride_axis=0)
            fwd_band[g * LANES : (g + 1) * LANES, 0:LANES] = jnp.where(col > row, turned, 0.0).astype(BF)
            fwd_band[g * LANES : (g + 1) * LANES, LANES : 2 * LANES] = jnp.where(
                col <= row, turned, 0.0
            ).astype(BF)
        before = halo[LANES:HALO, at].astype(F32)
        mixed = []
        for i in range(3):
            ext[0:8] = jnp.concatenate([jnp.zeros((6, LANES), F32), before[2 * i : 2 * i + 2]], axis=0)
            ext[8 : 8 + rows] = feats[i, :, at].astype(F32)
            mixed.append(
                taps[i : i + 1, at] * ext[8 : 8 + rows]
                + taps[3 + i : 4 + i, at] * ext[7 : 7 + rows]
                + taps[6 + i : 7 + i, at] * ext[6 : 6 + rows]
            )
        gate[:, at] = mixed[0]
        key[:, at] = mixed[1]
        value[:, at] = mixed[2]
        products = (mixed[1] * mixed[2]).astype(BF)
        first = jnp.concatenate([halo[0:LANES, at], products[:LANES]], axis=0)
        window = jnp.concatenate([first, products], axis=1)
        picked = pick_groups(
            jnp.dot(fwd_band[...], window, preferred_element_type=F32), per_tile, width
        )
        conv[0:LANES, at] = picked[:, :LANES]
        conv[LANES : 2 * LANES, at] = picked[:, LANES:]
        return carry

    lax.fori_loop(0, feats.shape[2] // LANES, tile, 0)


def forward_part(feats, taps, filters, halo):
    _, rows, channels = feats.shape
    groups = filters.shape[0]
    full = jax.ShapeDtypeStruct((rows, channels), F32)
    per_tile = groups * LANES // channels
    return pl.pallas_call(
        forward_kernel,
        out_shape=[full] * 4 + [jax.ShapeDtypeStruct((groups, LANES, 2 * LANES), BF)],
        in_specs=vmem(4),
        out_specs=vmem(5),
        scratch_shapes=[
            pltpu.VMEM((per_tile * LANES, 2 * LANES), BF),
            pltpu.VMEM((groups, LANES), F32),
            pltpu.VMEM((groups, LANES), F32),
            pltpu.VMEM((rows + 8, LANES), F32),
        ],
        compiler_params=params(8),
        cost_estimate=pl.CostEstimate(flops=2 << 30, bytes_accessed=12 << 20, transcendentals=0),
        name="forward_part",
    )(feats, taps, filters, halo)


def gated(own, last, conv, gate, grad_conv, grad_gate):
    grad_y = (own.astype(F32) + last[...].astype(F32)).astype(BF).astype(F32)
    down = (grad_y * gate).astype(BF)
    across = (grad_y * conv).astype(BF)
    grad_conv[...] = down
    grad_gate[...] = across
    return down, across


def head_kernel(own, last, conv, gate, feats, grad_conv, grad_gate, halo):
    down, across = gated(own[0:HEAD], last, conv[0:HEAD], gate[0:HEAD], grad_conv, grad_gate)
    halo[0:LANES] = down[0:LANES]
    pieces = [
        down[LANES:HEAD].astype(F32)[0:1],
        across[0:16].astype(F32)[0:2],
        feats[1, 0:16].astype(F32)[0:2],
        feats[2, 0:16].astype(F32)[0:2],
        jnp.zeros((9, down.shape[1]), F32),
    ]
    halo[LANES:HALO] = jnp.concatenate(pieces, axis=0).astype(BF)


def tail_gate_kernel(own, last, conv, gate, grad_conv, grad_gate):
    rows = conv.shape[0]
    gated(own[HEAD:rows], last, conv[HEAD:rows], gate[HEAD:rows], grad_conv, grad_gate)


def gate_head(own, last, conv, gate, feats):
    half = jax.ShapeDtypeStruct(last.shape, BF)
    return pl.pallas_call(
        head_kernel,
        out_shape=[half, half, jax.ShapeDtypeStruct((HALO, last.shape[1]), BF)],
        in_specs=vmem(5),
        out_specs=vmem(3),
        compiler_params=params(8),
        cost_estimate=pl.CostEstimate(flops=1 << 20, bytes_accessed=3 << 20, transcendentals=0),
        name="gate_head",
    )(own, last, conv, gate, feats)


def gate_tail(own, last, conv, gate):
    half = jax.ShapeDtypeStruct(last.shape, BF)
    return pl.pallas_call(
        tail_gate_kernel,
        out_shape=[half, half],
        in_specs=vmem(4),
        out_specs=vmem(2),
        compiler_params=params(8),
        cost_estimate=pl.CostEstimate(flops=1 << 20, bytes_accessed=3 << 20, transcendentals=0),
        name="gate_tail",
    )(own, last, conv, gate)


def final_kernel(
    conv_head, conv_tail, gate_head, gate_tail, halo, key, value, feats, taps, back, out, ext, small
):
    rows = key.shape[0]
    groups = back.shape[0]
    per_tile = groups * LANES // key.shape[1]
    width = LANES // per_tile

    def tile(l, carry):
        at = lane_tile(l)
        mine = jnp.concatenate([conv_head[:, at], conv_tail[:, at]], axis=0)
        after = halo[0:LANES, at]
        second = jnp.concatenate([mine[LANES:], after], axis=0)
        window = jnp.concatenate([mine, second], axis=1)
        first_group = pl.multiple_of(l * per_tile, per_tile)
        band = back[pl.ds(first_group, per_tile)]
        picked = pick_groups(
            jnp.dot(
                band.reshape(per_tile * LANES, 2 * LANES), window, preferred_element_type=F32
            ),
            per_tile,
            width,
        )
        rim = halo[LANES:HALO, at]
        beyond = jnp.concatenate([after, rim, jnp.zeros((LANES - 16, LANES), BF)], axis=0)
        top = band[:, 0:16, :].reshape(per_tile * 16, 2 * LANES)
        extra = pick_groups(jnp.dot(top, beyond, preferred_element_type=F32), per_tile, width)[0:2]
        rim_f = rim.astype(F32)
        streams = []
        for i, stream in ((1, value), (2, key)):
            other = 3 - i
            small[0:8] = feats[other, rows - 16 : rows, at].astype(F32)[8:16]
            small[8:16] = jnp.concatenate(
                [rim_f[1 + 2 * other : 3 + 2 * other], jnp.zeros((6, LANES), F32)], axis=0
            )
            beyond_mixed = (
                taps[other : other + 1, at] * small[8:10]
                + taps[3 + other : 4 + other, at] * small[7:9]
                + taps[6 + other : 7 + other, at] * small[6:8]
            )
            streams.append((i, stream, (extra * beyond_mixed).astype(BF).astype(F32)))

        def finish(i, mix_beyond):
            ext[rows : rows + 8] = jnp.concatenate([mix_beyond, jnp.zeros((6, LANES), F32)], axis=0)
            result = (
                taps[i : i + 1, at] * ext[0:rows]
                + taps[3 + i : 4 + i, at] * ext[1 : rows + 1]
                + taps[6 + i : 7 + i, at] * ext[2 : rows + 2]
            )
            out[i, :, at] = result.astype(BF)

        ext[0:HEAD] = gate_head[:, at].astype(F32)
        ext[HEAD:rows] = gate_tail[:, at].astype(F32)
        finish(0, rim_f[1:3])
        for i, stream, mix_beyond in streams:
            ext[0:LANES] = (picked[:, :LANES] * stream[0:LANES, at]).astype(BF).astype(F32)
            ext[LANES : 2 * LANES] = (
                (picked[:, LANES:] * stream[LANES : 2 * LANES, at]).astype(BF).astype(F32)
            )
            finish(i, mix_beyond)
        return carry

    lax.fori_loop(0, key.shape[1] // LANES, tile, 0)


def final_part(convs, gates, halo, key, value, feats, taps, back):
    rows, channels = key.shape
    return pl.pallas_call(
        final_kernel,
        out_shape=jax.ShapeDtypeStruct((3, rows, channels), BF),
        in_specs=vmem(10),
        out_specs=vmem(1)[0],
        scratch_shapes=[pltpu.VMEM((rows + 8, LANES), F32), pltpu.VMEM((16, LANES), F32)],
        compiler_params=params(8),
        cost_estimate=pl.CostEstimate(flops=2 << 30, bytes_accessed=12 << 20, transcendentals=0),
        name="final_part",
    )(*convs, *gates, halo, key, value, feats, taps, back)


def spread(quarters):
    flat = quarters.reshape((X * RING // 2,) + quarters.shape[2:])
    return lax.all_to_all(flat, ("x", "yq"), 0, 0).reshape(quarters.shape)


def local(features, short_taps, long_filters, out_weight, out_grad):
    feats = jnp.transpose(features[0], (1, 0, 2))
    _, channels = feats.shape[1:]
    taps = short_taps[0].reshape(9, channels)
    filters = jnp.transpose(long_filters[0])

    quarters = quarters_of(out_grad[0])
    weight = out_weight[0]
    b_held = gather_ring([weight[: channels // 2], weight[channels // 2 :]], "z")
    mine = spread(quarters)
    even = pair_ring(mine[: X // 2], ("yq", "yb"), 0)
    odd = pair_ring(mine[X // 2 :], ("yq", "yb"), 1)
    a_held = (mine, even, odd)
    halo_before = shift_ctx(tail_rows(feats, taps), 1, 1)
    feats = swap(feats)
    taps = swap(taps)
    filters = swap(filters)
    conv, gate, key, value, back = forward_part(feats, taps, filters, halo_before)

    send_head, a_head, a_tail, b_full = head_send(a_held, b_held)
    got_head = pair_x(send_head, 1, 0)
    send_tail = tail_send(a_tail, b_full)
    keep_head, keep_tail = kept(a_head, a_tail, b_full)
    got_tail = pair_x(send_tail, 3, 0)
    head, tail, own = fold(keep_head, got_head, keep_tail, got_tail)
    last_head = pair_x(head, 3, 1)
    last_tail = pair_x(tail, 1, 1)
    own = swap(own)
    conv_head, cross_head, halo = gate_head(own, last_head, conv, gate, feats)
    conv_tail, cross_tail = gate_tail(own, last_tail, conv, gate)
    halo_after = shift_ctx(halo, -1, 0)
    grad_feat = final_part(
        (conv_head, conv_tail), (cross_head, cross_tail), halo_after, key, value, feats, taps, back
    )
    return jnp.transpose(grad_feat, (1, 0, 2))[None]


def solution(mesh):
    parts = jax.sharding.Mesh(
        mesh.devices.reshape(RING, X, RING // 2, 2, 2),
        ("z", "x", "yq", "yb", "pp"),
        axis_types=(jax.sharding.AxisType.Auto,) * 5,
    )
    ctx, tp = ("z", "x"), ("yq", "yb")
    in_specs = (
        P("pp", ctx, None, tp),
        P("pp", None, None, tp),
        P("pp", None, tp),
        P("pp", tp, ctx),
        P("pp", ctx, tp),
    )
    out_specs = P("pp", ctx, None, tp)

    return jax.shard_map(local, mesh=parts, in_specs=in_specs, out_specs=out_specs, check_vma=False)
```
